32 devices in a mesh: row: 4 (over y, x), col: 8 (over z, core).
Axes of the slice: x: 2, y: 2, z: 4, core: 2. Of those that a mesh axis runs over, the one named last changes fastest.
Arguments:
- pair_repr: bfloat16 [1024, 1024, 128], P('row', 'col'), may hold values from -6 to 6
- logit_cotangent: bfloat16 [1024, 1024, 128], P('row', 'col'), may hold values from -6 to 6
- pair_mask: int32 [1024, 1024], P('row', 'col'), may hold values 0 or 1
- single_repr: bfloat16 [1024, 384], P(('row', 'col')), may hold values from -6 to 6
- token_index: int32 [1024], replicated, may hold values from 0 to 2046, as said below
- pair_up: bfloat16 [128, 512], replicated, may hold values from -0.5 to 0.5
- pair_gate: bfloat16 [128, 512], replicated, may hold values from -0.5 to 0.5
- pair_down: bfloat16 [512, 128], replicated, may hold values from -0.25 to 0.25
- head_weight: bfloat16 [128, 128], replicated, may hold values from -0.5 to 0.5
- rel_table: bfloat16 [65, 128], replicated, may hold values from -3 to 3
- proj_row: bfloat16 [384, 128], replicated, may hold values from -0.3125 to 0.3125
- proj_col: bfloat16 [384, 128], replicated, may hold values from -0.3125 to 0.3125
- single_gate: bfloat16 [384, 1536], replicated, may hold values from -0.3125 to 0.3125
- single_up: bfloat16 [384, 1536], replicated, may hold values from -0.3125 to 0.3125
- single_down: bfloat16 [1536, 384], replicated, may hold values from -0.15625 to 0.15625
Outputs:
- pair_grad: bfloat16 [1024, 1024, 128], P('row', 'col')
- single_grad: bfloat16 [1024, 384], P(('row', 'col'))
- grad_pair_up: float32 [128, 512], replicated
- grad_pair_gate: float32 [128, 512], replicated
- grad_pair_down: float32 [512, 128], replicated
- grad_head: float32 [128, 128], replicated
- grad_rel: float32 [65, 128], replicated
- grad_proj_row: float32 [384, 128], replicated
- grad_proj_col: float32 [384, 128], replicated
- grad_single_gate: float32 [384, 1536], P(None, ('row', 'col'))
- grad_single_up: float32 [384, 1536], P(None, ('row', 'col'))
- grad_single_down: float32 [1536, 384], P(('row', 'col'))
The draws below stay inside these ranges and needn't reach their ends.
Inputs may be any that keep to these rules, and one draw needn't show every extreme that they name: `token_index`: strictly increasing, entry 0 is 0, successive entries differ by 1 to 3, the last entry is 2046.
All inputs are finite; a program needn't handle non-finite values. No bound on the sum of `pair_mask` on one device may be relied on, other than what follows from the above.
Results may differ from the reference program's by a relative error of at most 0.018.
Values may be sent and summed in bfloat16 or wider, within the bound.
No kernel may reach another device: no remote copies, remote signals or barrier semaphores. Data moves between devices by JAX's collectives and lax.ppermute only.
A program may use at most 192 MiB of HBM per device.

```python
import jax
import jax.numpy as jnp
from jax import lax

CZ = 128
HID = 512
NB = 64
CS = 384
SH = 1536
NREL = 65
TOKENS = 1024


def draw_token_index(key, part):
    places = jnp.arange(TOKENS, dtype=jnp.int32)
    shifts = jax.random.randint(key, (TOKENS,), -1, 1)
    ends = (places == 0) | (places == TOKENS - 1)
    shifts = jnp.where(ends, 0, shifts)
    return (2 * places + shifts).astype(jnp.int32)


def touch_ends(entries, own_key, low, largest):
    index_at = [jax.random.randint(jax.random.fold_in(own_key, axis), (), 0, length) for axis, length in enumerate(entries.shape)]
    main_axis = entries.shape.index(max(entries.shape))
    beside = index_at[:main_axis] + [(index_at[main_axis] + 1) % entries.shape[main_axis]] + index_at[main_axis + 1:]
    return entries.at[tuple(index_at)].set(low).at[tuple(beside)].set(largest)


def levels(stream_key, shape, shards, least, largest):
    def one(dim, parts):
        draws = jax.random.uniform(jax.random.fold_in(jax.random.fold_in(stream_key, 6), dim), (parts,), jnp.float32, least / len(shards), largest / len(shards))
        return jnp.repeat(jnp.exp(draws), shape[dim] // parts).reshape((-1,) + (1,) * (len(shape) - dim - 1))

    loudness = one(*shards[0])
    for cut in shards[1:]:
        loudness = loudness * one(*cut)
    return loudness


def noise(stream_key, shape, scale, limit, cuts=(), held_as=jnp.bfloat16):
    gain = levels(stream_key, shape, cuts, -0.22, 0.18) if cuts else 1.0
    array = jax.random.normal(stream_key, shape, jnp.float32) * scale * gain
    return jnp.minimum(jnp.maximum(array, -limit), limit).astype(held_as)


def setup_inputs(seed: int = 0) -> dict:
    keys = jax.random.split(jax.random.key(seed), 16)
    pair_repr = noise(keys[0], (TOKENS, TOKENS, CZ), 1.0, 6.0, ((0, 4), (1, 8)))
    logit_cotangent = noise(keys[1], (TOKENS, TOKENS, 2 * NB), 1.0, 6.0, ((0, 4), (1, 8)))
    pair_mask = touch_ends((jax.random.randint(keys[2], (TOKENS, TOKENS), 0, 8) < 7).astype(jnp.int32), jax.random.fold_in(keys[2], 1), 0, 1)
    single_repr = noise(keys[3], (TOKENS, CS), 1.0, 6.0, ((0, 32),))
    token_index = draw_token_index(jax.random.fold_in(keys[15], 71), 0)
    pair_up = noise(keys[5], (CZ, HID), CZ ** -0.5, 0.5)
    pair_gate = noise(keys[6], (CZ, HID), CZ ** -0.5, 0.5)
    pair_down = noise(keys[7], (HID, CZ), HID ** -0.5, 0.25)
    head_weight = noise(keys[8], (CZ, 2 * NB), CZ ** -0.5, 0.5)
    rel_table = noise(keys[9], (NREL, CZ), 0.5, 3.0)
    proj_row = noise(keys[10], (CS, CZ), CS ** -0.5, 0.3125)
    proj_col = noise(keys[11], (CS, CZ), CS ** -0.5, 0.3125)
    single_gate = noise(keys[12], (CS, SH), CS ** -0.5, 0.3125)
    single_up = noise(keys[13], (CS, SH), CS ** -0.5, 0.3125)
    single_down = noise(keys[14], (SH, CS), SH ** -0.5, 0.15625)
    return {"pair_repr": pair_repr, "logit_cotangent": logit_cotangent, "pair_mask": pair_mask, "single_repr": single_repr, "token_index": token_index, "pair_up": pair_up, "pair_gate": pair_gate, "pair_down": pair_down, "head_weight": head_weight, "rel_table": rel_table, "proj_row": proj_row, "proj_col": proj_col, "single_gate": single_gate, "single_up": single_up, "single_down": single_down}


norm_eps = 1e-05

def gated_parts(gate):
    sigma = jax.nn.sigmoid(gate)
    return (gate * sigma, sigma * (1.0 + gate * (1.0 - sigma)))

def product(matrix_a, matrix_b):
    return jnp.dot(matrix_a, matrix_b, preferred_element_type=jnp.float32)

def product_left(matrix_a, matrix_b):
    return lax.dot_general(matrix_a, matrix_b, (((0,), (0,)), ((), ())), preferred_element_type=jnp.float32)

def product_right(matrix_a, matrix_b):
    return lax.dot_general(matrix_a, matrix_b, (((1,), (1,)), ((), ())), preferred_element_type=jnp.float32)

def single_forward(single_repr, single_gate, single_up, single_down):
    source = single_repr.astype(jnp.float32)
    inverse_rms = lax.rsqrt(lax.optimization_barrier(jnp.mean(source * source, axis=-1, keepdims=True)) + norm_eps)
    normed = source * inverse_rms
    normed_bf = normed.astype(jnp.bfloat16)
    gate_pre = product(normed_bf, single_gate)
    up_pre = product(normed_bf, single_up)
    silu_value, silu_slope = gated_parts(gate_pre)
    hidden = (silu_value * up_pre).astype(jnp.bfloat16)
    updated = (source + product(hidden, single_down)).astype(jnp.bfloat16)
    return (normed, inverse_rms, normed_bf, up_pre, silu_value, silu_slope, hidden, updated)

def single_backward(grad_in, saved_state, single_gate, single_up, single_down):
    normed, inverse_rms, normed_bf, up_pre, silu_value, silu_slope, hidden, updated = saved_state
    grad_bf = grad_in.astype(jnp.bfloat16)
    down_sum = product_left(hidden, grad_bf)
    grad_hidden = product_right(grad_bf, single_down)
    grad_up = (grad_hidden * silu_value).astype(jnp.bfloat16)
    grad_gate = (grad_hidden * up_pre * silu_slope).astype(jnp.bfloat16)
    gate_sum = product_left(normed_bf, grad_gate)
    up_sum = product_left(normed_bf, grad_up)
    grad_normed = product_right(grad_gate, single_gate) + product_right(grad_up, single_up)
    grad_source = grad_in + inverse_rms * (grad_normed - normed * lax.optimization_barrier(jnp.mean(grad_normed * normed, axis=-1, keepdims=True)))
    return (grad_source, gate_sum, up_sum, down_sum)

def pair_block(pair_blk, cot_blk, mirror_blk, row_blk, col_blk, row_pos, col_pos, rel_table, up_gate, pair_down, head_weight):
    n_rows, n_cols, pair_width = pair_blk.shape
    bin_count = mirror_blk.shape[2]
    rel_count = rel_table.shape[0]
    rel_span = (rel_count - 1) // 2
    pair_count = n_rows * n_cols
    offset = jnp.clip(row_pos[:, None] - col_pos[None, :], -rel_span, rel_span) + rel_span
    one_hot = offset.reshape(pair_count, 1) == jnp.arange(rel_count, dtype=jnp.int32)[None, :]
    hot_table = one_hot.astype(jnp.bfloat16)
    pair_in = pair_blk.astype(jnp.float32) + row_blk.astype(jnp.float32)[:, None, :] + col_blk.astype(jnp.float32)[None, :, :]
    pair_in = pair_in.reshape(pair_count, pair_width) + product(hot_table, rel_table)
    centred = pair_in - lax.optimization_barrier(jnp.mean(pair_in, axis=-1, keepdims=True))
    inv_std = lax.rsqrt(lax.optimization_barrier(jnp.mean(centred * centred, axis=-1, keepdims=True)) + norm_eps)
    normed = centred * inv_std
    normed_bf = normed.astype(jnp.bfloat16)
    hidden_width = up_gate.shape[1] // 2
    both_pre = product(normed_bf, up_gate)
    up_pre = both_pre[:, :hidden_width]
    gate_pre = both_pre[:, hidden_width:]
    silu_value, silu_slope = gated_parts(gate_pre)
    hidden = (silu_value * up_pre).astype(jnp.bfloat16)
    pair_out = (pair_in + product(hidden, pair_down)).astype(jnp.bfloat16)
    cot_flat = cot_blk.reshape(pair_count, 2 * bin_count)
    symmetric = (cot_flat[:, bin_count:].astype(jnp.float32) + mirror_blk.reshape(pair_count, bin_count).astype(jnp.float32)).astype(jnp.bfloat16)
    head_cot = jnp.concatenate([cot_flat[:, :bin_count], symmetric], axis=1)
    grad_out = product_right(head_cot, head_weight)
    grad_out_bf = grad_out.astype(jnp.bfloat16)
    grad_hidden = product_right(grad_out_bf, pair_down)
    grad_both = jnp.concatenate([(grad_hidden * silu_value).astype(jnp.bfloat16), (grad_hidden * up_pre * silu_slope).astype(jnp.bfloat16)], axis=1)
    grad_normed = product_right(grad_both, up_gate)
    grad_in = grad_out + inv_std * (grad_normed - lax.optimization_barrier(jnp.mean(grad_normed, axis=-1, keepdims=True)) - normed * lax.optimization_barrier(jnp.mean(grad_normed * normed, axis=-1, keepdims=True)))
    head_sum = product_left(pair_out, head_cot)
    down_sum = product_left(hidden, grad_out_bf)
    up_gate_sum = product_left(normed_bf, grad_both)
    rel_sum = lax.dot_general(one_hot.astype(jnp.float32), grad_in, (((0,), (0,)), ((), ())), precision=lax.Precision.HIGHEST, preferred_element_type=jnp.float32)
    grad_tile = grad_in.reshape(n_rows, n_cols, pair_width)
    return (grad_tile.astype(jnp.bfloat16), lax.optimization_barrier(jnp.sum(grad_tile, axis=1)), lax.optimization_barrier(jnp.sum(grad_tile, axis=0)), up_gate_sum, down_sum, head_sum, rel_sum)

def reference(pair_repr, logit_cotangent, pair_mask, single_repr, token_index, pair_up, pair_gate, pair_down, head_weight, rel_table, proj_row, proj_col, single_gate, single_up, single_down):
    saved_state = single_forward(single_repr, single_gate, single_up, single_down)
    updated = saved_state[7]
    row_proj = product(updated, proj_row).astype(jnp.bfloat16)
    col_proj = product(updated, proj_col).astype(jnp.bfloat16)
    masked = logit_cotangent * pair_mask[:, :, None].astype(jnp.bfloat16)
    mirrored = jnp.swapaxes(masked[:, :, NB:], 0, 1)
    up_gate = jnp.concatenate([pair_up, pair_gate], axis=1)
    block_rows = 64
    n_blocks = TOKENS // block_rows

    def block_step(running, inputs):
        pair_blk, cot_blk, mirror_blk, row_blk, pos_blk = inputs
        grad_blk, row_sum, col_sum, up_gate_sum, down_sum, head_sum, rel_sum = pair_block(pair_blk, cot_blk, mirror_blk, row_blk, col_proj, pos_blk, token_index, rel_table, up_gate, pair_down, head_weight)
        running = (running[0] + col_sum, running[1] + up_gate_sum, running[2] + down_sum, running[3] + head_sum, running[4] + rel_sum)
        return (running, (grad_blk, row_sum))
    initial = (jnp.zeros((TOKENS, CZ), jnp.float32), jnp.zeros((CZ, 2 * HID), jnp.float32), jnp.zeros((HID, CZ), jnp.float32), jnp.zeros((CZ, 2 * NB), jnp.float32), jnp.zeros((NREL, CZ), jnp.float32))
    sliced = (pair_repr.reshape(n_blocks, block_rows, TOKENS, CZ), masked.reshape(n_blocks, block_rows, TOKENS, 2 * NB), mirrored.reshape(n_blocks, block_rows, TOKENS, NB), row_proj.reshape(n_blocks, block_rows, CZ), token_index.reshape(n_blocks, block_rows))
    sums_out, blocks_out = lax.scan(block_step, initial, sliced)
    col_total, up_gate_sum, down_sum, head_sum, rel_sum = sums_out
    grad_blocks, row_sums = blocks_out
    pair_grad = grad_blocks.reshape(TOKENS, TOKENS, CZ)
    row_bf = row_sums.reshape(TOKENS, CZ).astype(jnp.bfloat16)
    col_bf = col_total.astype(jnp.bfloat16)
    single_cot = product_right(row_bf, proj_row) + product_right(col_bf, proj_col)
    prow_sum = product_left(updated, row_bf)
    pcol_sum = product_left(updated, col_bf)
    grad_source, gate_sum, up_sum, sdown_sum = single_backward(single_cot, saved_state, single_gate, single_up, single_down)
    grad_scale = 1.0 / TOKENS
    return (pair_grad, grad_source.astype(jnp.bfloat16), up_gate_sum[:, :HID] * grad_scale, up_gate_sum[:, HID:] * grad_scale, down_sum * grad_scale, head_sum * grad_scale, rel_sum * grad_scale, prow_sum * grad_scale, pcol_sum * grad_scale, gate_sum * grad_scale, up_sum * grad_scale, sdown_sum * grad_scale)
```

```python
import functools

import jax
import jax.numpy as jnp
from jax import lax
from jax.experimental import pallas as pl
from jax.experimental.pallas import tpu as pltpu
from jax.sharding import PartitionSpec as P


norm_eps = 1e-05
lanes = 128
axes = ("row", "col")
f32 = jnp.float32
bf16 = jnp.bfloat16


def gated_parts(gate):
    sigma = jax.nn.sigmoid(gate)
    return (gate * sigma, sigma * (1.0 + gate * (1.0 - sigma)))


def product(matrix_a, matrix_b):
    return jnp.dot(matrix_a, matrix_b, preferred_element_type=f32)


def product_left(matrix_a, matrix_b):
    return lax.dot_general(matrix_a, matrix_b, (((0,), (0,)), ((), ())), preferred_element_type=f32)


def product_right(matrix_a, matrix_b):
    return lax.dot_general(matrix_a, matrix_b, (((1,), (1,)), ((), ())), preferred_element_type=f32)


def forward_kernel(
    span, pair_ref, row_ref, col_ref, rpos_ref, cpos_ref, table_ref, up_gate_ref, down_ref,
    hid_ref, silu_ref, slope_ref, norm_ref, norm_t_ref, inv_ref, out_t_ref,
):
    n_rows, n_cols, width = pair_ref.shape
    count = n_rows * n_cols
    hidden = down_ref.shape[0]
    offset = jnp.clip(rpos_ref[...][:, None, :] - cpos_ref[...][None, :, :], -span, span) + span
    lane = lax.broadcasted_iota(jnp.int32, offset.shape, 2)
    hot = jnp.where(offset == lane, 1.0, 0.0).astype(bf16).reshape(count, lanes)
    pair_in = pair_ref[...].astype(f32) + row_ref[...][:, None, :] + col_ref[...][None, :, :]
    pair_in = pair_in.reshape(count, width) + product(hot, table_ref[...])
    centred = pair_in - jnp.mean(pair_in, axis=-1, keepdims=True)
    inv_std = lax.rsqrt(jnp.mean(centred * centred, axis=-1, keepdims=True) + norm_eps)
    normed = centred * inv_std
    normed_bf = normed.astype(bf16)
    norm_ref[...] = normed_bf
    norm_t_ref[0] = normed_bf.T
    inv_ref[...] = jnp.broadcast_to(inv_std, (count, width)).astype(bf16)
    both = product(normed_bf, up_gate_ref[...])
    up_pre = both[:, :hidden]
    gate_pre = both[:, hidden:]
    sigma = 0.5 * jnp.tanh(0.5 * gate_pre) + 0.5
    silu = gate_pre * sigma
    hid = (silu * up_pre).astype(bf16)
    hid_ref[...] = hid
    silu_ref[...] = silu.astype(bf16)
    slope_ref[...] = (up_pre * (sigma + silu * (1.0 - sigma))).astype(bf16)
    pair_out = (pair_in + product(hid, down_ref[...])).astype(bf16)
    out_t_ref[0] = pair_out.T


def backward_kernel(
    n_pieces, n_given, idx_ref, masked_ref, *refs
):
    mirror_refs = refs[:n_pieces]
    (hid_ref, silu_ref, slope_ref, norm_ref, norm_t_ref, inv_ref, out_t_ref, bucket_ref,
     head_t_ref, down_t_ref, up_t_ref, gate_t_ref) = refs[n_pieces:n_pieces + 12]
    refs = refs[n_pieces + 12 + n_given:]
    grad_ref, rows_ref, cols_ref, sums_ref, mir_ref, ug_acc, down_acc, head_acc, rel_acc = refs
    piece = pl.program_id(0)
    step = pl.program_id(1)
    first = (piece == 0) & (step == 0)
    last = (piece == pl.num_programs(0) - 1) & (step == pl.num_programs(1) - 1)
    n_rows, n_cols, width = masked_ref.shape
    count = n_rows * n_cols
    half = n_cols // 2
    hidden = down_t_ref.shape[1]
    bins = width // 2

    @pl.when(first)
    def _():
        cols_ref[...] = jnp.zeros_like(cols_ref)
        ug_acc[...] = jnp.zeros_like(ug_acc)
        down_acc[...] = jnp.zeros_like(down_acc)
        head_acc[...] = jnp.zeros_like(head_acc)
        rel_acc[...] = jnp.zeros_like(rel_acc)

    for t in range(n_pieces):
        @pl.when(piece == t)
        def _(t=t):
            mir_ref[...] = mirror_refs[t][...]

    packed = mir_ref[...].astype(f32).reshape(n_rows * half, width)
    turned = pltpu.roll(packed, bins, 1).reshape(n_rows, half, width)
    mirrored = jnp.concatenate([turned, packed.reshape(n_rows, half, width)], axis=1)
    lane = lax.broadcasted_iota(jnp.int32, mirrored.shape, 2)
    own = masked_ref[...].astype(f32)
    head_cot = (own + jnp.where(lane >= bins, mirrored, 0.0)).astype(bf16).reshape(count, width)
    grad_out = product(head_cot, head_t_ref[...])
    grad_out_bf = grad_out.astype(bf16)
    grad_hid = product(grad_out_bf, down_t_ref[...]).astype(bf16)
    grad_up = grad_hid * silu_ref[...]
    grad_gate = grad_hid * slope_ref[...]
    grad_normed = product(grad_up, up_t_ref[...]) + product(grad_gate, gate_t_ref[...])
    normed = norm_ref[...].astype(f32)
    grad_in = grad_out + inv_ref[...].astype(f32) * (
        grad_normed
        - jnp.mean(grad_normed, axis=-1, keepdims=True)
        - normed * jnp.mean(grad_normed * normed, axis=-1, keepdims=True)
    )
    grad_tile = grad_in.reshape(n_rows, n_cols, width)
    grad_bf = grad_in.astype(bf16)
    grad_ref[...] = grad_bf.reshape(n_rows, n_cols, width)
    rows_ref[...] = jnp.sum(grad_tile, axis=1)
    cols_ref[...] += jnp.sum(grad_tile, axis=0)
    norm_t = norm_t_ref[0]
    ug_acc[:, :hidden] += product(norm_t, grad_up)
    ug_acc[:, hidden:] += product(norm_t, grad_gate)
    down_acc[...] += product(grad_out_bf.T, hid_ref[...])
    head_acc[...] += product(out_t_ref[0], head_cot)
    level = lax.broadcasted_iota(jnp.int32, (lanes, count), 0)
    hot_t = jnp.where(jnp.broadcast_to(bucket_ref[0], (lanes, count)) == level, 1.0, 0.0).astype(bf16)
    rel_acc[...] += product(hot_t, grad_bf)

    @pl.when(last)
    def _():
        n_slabs = hidden // lanes
        for q in range(2 * n_slabs):
            sums_ref[q] = ug_acc[:, q * lanes:(q + 1) * lanes]
        for q in range(n_slabs):
            sums_ref[2 * n_slabs + q] = down_acc[:, q * lanes:(q + 1) * lanes].T
        sums_ref[3 * n_slabs] = head_acc[...]
        sums_ref[3 * n_slabs + 1] = rel_acc[...]
        for q in range(3 * n_slabs + 2, sums_ref.shape[0]):
            sums_ref[q] = jnp.zeros((lanes, lanes), f32)


def gather_all(piece, n_dev):
    copies = jnp.broadcast_to(piece[None], (n_dev,) + piece.shape)
    return lax.all_to_all(copies, axes, split_axis=0, concat_axis=0, tiled=True)


def local(
    pair_repr, logit_cotangent, pair_mask, single_repr, token_index, pair_up, pair_gate, pair_down, head_weight,
    rel_table, proj_row, proj_col, single_gate, single_up, single_down,
):
    n_row = lax.axis_size("row")
    n_col = lax.axis_size("col")
    n_dev = n_row * n_col
    fold = n_col // n_row
    row_index = lax.axis_index("row")
    col_index = lax.axis_index("col")
    joint_index = row_index * n_col + col_index
    core = col_index % fold
    tile_rows, tile_cols, width = pair_repr.shape
    bins = width // 2
    half = tile_cols // 2
    strip = single_repr.shape[0]
    tokens = strip * n_dev
    hidden = pair_up.shape[1]
    s_hidden = single_gate.shape[1]
    share = s_hidden // n_dev
    n_rel = rel_table.shape[0]
    span = (n_rel - 1) // 2
    n_chunks = 2
    per_turn = n_row // fold
    piece_rows = tile_cols // n_chunks // per_turn
    block_rows = min(1024 // tile_cols, piece_rows)
    count = block_rows * tile_cols
    n_blocks = tile_rows // block_rows
    n_slabs = hidden // lanes
    n_sums = 4 * n_slabs

    masked = logit_cotangent * pair_mask[:, :, None].astype(bf16)
    source = masked[:, :, bins:].reshape(fold, 2, half, tile_cols, bins)
    source = source.transpose(0, 3, 2, 1, 4).reshape(fold, tile_cols, half, width)
    turns = [lax.dynamic_index_in_dim(source, (core + s) % fold, 0, keepdims=False) for s in range(fold)]

    def place(r, k, b):
        return r * n_col + k * fold + b

    every = [(r, k, b) for r in range(n_row) for k in range(n_row) for b in range(fold)]
    pieces = {}
    for chunk in range(n_chunks):
        for t in range(n_row):
            s, part = t // per_turn, t % per_turn
            start = (chunk * per_turn + part) * piece_rows
            sent = lax.slice_in_dim(turns[s], start, start + piece_rows, axis=0)
            spread = [(place(r, k, b), place((r + k + t) % n_row, k, b)) for r, k, b in every]
            pieces[chunk, t] = lax.ppermute(sent, axes, spread)
    singles = gather_all(single_repr, n_dev).reshape(tokens, -1)
    for chunk in range(n_chunks):
        for t in range(n_row):
            s = t // per_turn
            onward = [
                (place((r + k + t) % n_row, k, b), place(k, r, (b + s) % fold)) for r, k, b in every
            ]
            pieces[chunk, t] = lax.ppermute(pieces[chunk, t], axes, onward)

    src = singles.astype(f32)
    inv_rms = lax.rsqrt(jnp.mean(src * src, axis=-1, keepdims=True) + norm_eps)
    s_normed = src * inv_rms
    s_normed_bf = s_normed.astype(bf16)
    s_silu, _ = gated_parts(product(s_normed_bf, single_gate))
    s_hid = (s_silu * product(s_normed_bf, single_up)).astype(bf16)
    updated = (src + product(s_hid, single_down)).astype(bf16)
    row_tokens = lax.dynamic_slice_in_dim(updated, row_index * tile_rows, tile_rows, 0)
    col_tokens = lax.dynamic_slice_in_dim(updated, col_index * tile_cols, tile_cols, 0)
    row_proj = product(row_tokens, proj_row).astype(bf16).astype(f32)
    col_proj = product(col_tokens, proj_col).astype(bf16).astype(f32)

    row_pos = lax.dynamic_slice_in_dim(token_index, row_index * tile_rows, tile_rows, 0)
    col_pos = lax.dynamic_slice_in_dim(token_index, col_index * tile_cols, tile_cols, 0)
    rpos = jnp.broadcast_to(row_pos[:, None], (tile_rows, lanes))
    cpos = jnp.broadcast_to(col_pos[:, None], (tile_cols, lanes))
    bucket = (jnp.clip(row_pos[:, None] - col_pos[None, :], -span, span) + span).reshape(n_blocks, 1, count)
    table = jnp.pad(rel_table, ((0, lanes - n_rel), (0, 0)))
    up_gate = jnp.concatenate([pair_up, pair_gate], axis=1)

    n_pairs = tile_rows * tile_cols
    whole = lambda shape: pl.BlockSpec(shape, lambda *_: (0,) * len(shape))
    fwd_flops = 2 * n_pairs * width * (3 * hidden + lanes)
    saved = pl.pallas_call(
        functools.partial(forward_kernel, span),
        grid=(n_blocks,),
        in_specs=[
            pl.BlockSpec((block_rows, tile_cols, width), lambda i: (i, 0, 0)),
            pl.BlockSpec((block_rows, width), lambda i: (i, 0)),
            whole((tile_cols, width)),
            pl.BlockSpec((block_rows, lanes), lambda i: (i, 0)),
            whole((tile_cols, lanes)),
            whole(table.shape),
            whole(up_gate.shape),
            whole(pair_down.shape),
        ],
        out_specs=[
            pl.BlockSpec((count, hidden), lambda i: (i, 0)),
            pl.BlockSpec((count, hidden), lambda i: (i, 0)),
            pl.BlockSpec((count, hidden), lambda i: (i, 0)),
            pl.BlockSpec((count, width), lambda i: (i, 0)),
            pl.BlockSpec((1, width, count), lambda i: (i, 0, 0)),
            pl.BlockSpec((count, width), lambda i: (i, 0)),
            pl.BlockSpec((1, width, count), lambda i: (i, 0, 0)),
        ],
        out_shape=[
            jax.ShapeDtypeStruct((n_pairs, hidden), bf16),
            jax.ShapeDtypeStruct((n_pairs, hidden), bf16),
            jax.ShapeDtypeStruct((n_pairs, hidden), bf16),
            jax.ShapeDtypeStruct((n_pairs, width), bf16),
            jax.ShapeDtypeStruct((n_blocks, width, count), bf16),
            jax.ShapeDtypeStruct((n_pairs, width), bf16),
            jax.ShapeDtypeStruct((n_blocks, width, count), bf16),
        ],
        cost_estimate=pl.CostEstimate(
            flops=fwd_flops, bytes_accessed=n_pairs * (6 * hidden + 10 * width), transcendentals=n_pairs * hidden
        ),
        name="pair_forward",
    )(pair_repr, row_proj, col_proj, rpos, cpos, table, up_gate, pair_down)

    head_t = head_weight.T
    down_t = pair_down.T
    up_t = pair_up.T
    gate_t = pair_gate.T
    steps = piece_rows // block_rows
    given = ()
    sums, cols = 0.0, 0.0
    core_arr = core.astype(jnp.int32).reshape(1)
    for chunk in range(n_chunks):
        def block_of(t, j, idx, chunk=chunk):
            strip_no = (idx[0] + fold - t // per_turn) % fold
            return strip_no * (tile_cols // block_rows) + (chunk * per_turn + t % per_turn) * steps + j

        def mirror_map(t, j, idx, own=0):
            return (jnp.where(t == own, j, jnp.where(t < own, 0, steps - 1)), 0, 0)

        flat = lambda cols_: pl.BlockSpec((count, cols_), lambda t, j, idx: (block_of(t, j, idx), 0))
        lead = lambda shape: pl.BlockSpec((1,) + shape, lambda t, j, idx: (block_of(t, j, idx), 0, 0))
        tile = pl.BlockSpec((block_rows, tile_cols, width), lambda t, j, idx: (block_of(t, j, idx), 0, 0))
        rows_spec = pl.BlockSpec((block_rows, width), lambda t, j, idx: (block_of(t, j, idx), 0))
        in_specs = (
            [tile]
            + [
                pl.BlockSpec((block_rows, half, width), functools.partial(mirror_map, own=t))
                for t in range(n_row)
            ]
            + [flat(hidden), flat(hidden), flat(hidden), flat(width), lead((width, count)), flat(width),
               lead((width, count)), lead((1, count)),
               whole(head_t.shape), whole(down_t.shape), whole(up_t.shape), whole(gate_t.shape)]
            + [pl.BlockSpec(memory_space=pl.ANY)] * len(given)
        )
        operands = [masked] + [pieces[chunk, t] for t in range(n_row)] + list(saved) + [
            bucket, head_t, down_t, up_t, gate_t] + list(given)
        first_given = 1 + len(operands) - len(given)
        pair_grad, row_part, col_part, sum_part = pl.pallas_call(
            functools.partial(backward_kernel, n_row, len(given)),
            grid_spec=pltpu.PrefetchScalarGridSpec(
                num_scalar_prefetch=1,
                grid=(n_row, steps),
                in_specs=in_specs,
                out_specs=[tile, rows_spec, whole((tile_cols, width)), whole((n_sums, lanes, lanes))],
                scratch_shapes=[
                    pltpu.VMEM((block_rows, half, width), bf16),
                    pltpu.VMEM((width, 2 * hidden), f32),
                    pltpu.VMEM((width, hidden), f32),
                    pltpu.VMEM((width, lanes), f32),
                    pltpu.VMEM((lanes, width), f32),
                ],
            ),
            out_shape=[
                jax.ShapeDtypeStruct(pair_repr.shape, bf16),
                jax.ShapeDtypeStruct((tile_rows, width), f32),
                jax.ShapeDtypeStruct((tile_cols, width), f32),
                jax.ShapeDtypeStruct((n_sums, lanes, lanes), f32),
            ],
            input_output_aliases={first_given + i: i for i in range(len(given))},
            cost_estimate=pl.CostEstimate(
                flops=2 * n_pairs * width * (6 * hidden + 3 * lanes) // n_chunks,
                bytes_accessed=n_pairs * (6 * hidden + 13 * width) // n_chunks,
                transcendentals=0,
            ),
            name="pair_backward",
        )(core_arr, *operands)
        given = (pair_grad, row_part)
        sums = sums + sum_part
        cols = cols + col_part

    at_row = lax.broadcasted_iota(jnp.int32, (n_row, n_col, 1, 1), 0) == row_index
    at_col = lax.broadcasted_iota(jnp.int32, (n_row, n_col, 1, 1), 1) == col_index
    row_sent = jnp.where(at_row, row_part.reshape(1, n_col, strip, width), 0.0)
    col_sent = jnp.where(at_col, cols.reshape(n_row, 1, strip, width), 0.0)
    sum_rows = n_sums * lanes // n_dev
    outgoing = jnp.concatenate(
        [
            sums.reshape(n_dev, sum_rows, lanes).astype(bf16),
            row_sent.reshape(n_dev, strip, width).astype(bf16),
            col_sent.reshape(n_dev, strip, width).astype(bf16),
        ],
        axis=1,
    )
    arrived = lax.all_to_all(outgoing, axes, split_axis=0, concat_axis=0, tiled=True)
    reduced = jnp.sum(arrived.astype(f32), axis=0)
    grad_scale = 1.0 / tokens
    scales = jnp.where(jnp.arange(reduced.shape[0])[:, None] < sum_rows, grad_scale, 1.0)
    everywhere = gather_all((reduced * scales).astype(bf16), n_dev).reshape(n_dev, sum_rows + 2 * strip, lanes)
    slabs = everywhere[:, :sum_rows].reshape(n_sums, lanes, lanes).astype(f32)
    row_bf = everywhere[:, sum_rows:sum_rows + strip].reshape(tokens, width)
    col_bf = everywhere[:, sum_rows + strip:].reshape(n_row, n_col, strip, width)
    col_bf = col_bf.transpose(1, 0, 2, 3).reshape(tokens, width)

    single_cot = product_right(row_bf, proj_row) + product_right(col_bf, proj_col)
    cot_bf = single_cot.astype(bf16)
    prow_sum = product_left(updated, row_bf)
    pcol_sum = product_left(updated, col_bf)
    gate_cols = lax.dynamic_slice_in_dim(single_gate, joint_index * share, share, 1)
    up_cols = lax.dynamic_slice_in_dim(single_up, joint_index * share, share, 1)
    down_rows = lax.dynamic_slice_in_dim(single_down, joint_index * share, share, 0)
    own_up = product(s_normed_bf, up_cols)
    own_silu, own_slope = gated_parts(product(s_normed_bf, gate_cols))
    own_hid = (own_silu * own_up).astype(bf16)
    own_grad_hid = product_right(cot_bf, down_rows)
    own_grad_up = (own_grad_hid * own_silu).astype(bf16)
    own_grad_gate = (own_grad_hid * own_up * own_slope).astype(bf16)
    gate_sum = product_left(s_normed_bf, own_grad_gate)
    up_sum = product_left(s_normed_bf, own_grad_up)
    down_sum = product_left(own_hid, cot_bf)

    mine = lambda whole_: lax.dynamic_slice_in_dim(whole_, joint_index * strip, strip, 0)
    my_src = single_repr.astype(f32)
    my_inv = lax.rsqrt(jnp.mean(my_src * my_src, axis=-1, keepdims=True) + norm_eps)
    my_normed = my_src * my_inv
    my_normed_bf = my_normed.astype(bf16)
    my_up = product(my_normed_bf, single_up)
    my_silu, my_slope = gated_parts(product(my_normed_bf, single_gate))
    my_cot = mine(single_cot)
    my_grad_hid = product_right(my_cot.astype(bf16), single_down)
    my_grad_up = (my_grad_hid * my_silu).astype(bf16)
    my_grad_gate = (my_grad_hid * my_up * my_slope).astype(bf16)
    my_grad_normed = product_right(my_grad_gate, single_gate) + product_right(my_grad_up, single_up)
    single_grad = my_cot + my_inv * (
        my_grad_normed - my_normed * jnp.mean(my_grad_normed * my_normed, axis=-1, keepdims=True)
    )

    def wide(first):
        return slabs[first:first + n_slabs].transpose(1, 0, 2).reshape(width, hidden)

    return (
        pair_grad,
        single_grad.astype(bf16),
        wide(0),
        wide(n_slabs),
        slabs[2 * n_slabs:3 * n_slabs].reshape(hidden, width),
        slabs[3 * n_slabs],
        slabs[3 * n_slabs + 1][:n_rel],
        prow_sum * grad_scale,
        pcol_sum * grad_scale,
        gate_sum * grad_scale,
        up_sum * grad_scale,
        down_sum * grad_scale,
    )


def solution(mesh):
    placed = (
        P("row", "col", None),
        P("row", "col", None),
        P("row", "col"),
        P(("row", "col"), None),
    ) + (P(),) * 11
    return jax.shard_map(
        local,
        mesh=mesh,
        in_specs=placed,
        out_specs=(P("row", "col", None), P(("row", "col"), None))
        + (P(),) * 7
        + (P(None, ("row", "col")), P(None, ("row", "col")), P(("row", "col"), None)),
        check_vma=False,
    )
```

```python
import functools

import jax
import jax.numpy as jnp
from jax import lax
from jax.experimental import pallas as pl
from jax.experimental.pallas import tpu as pltpu
from jax.sharding import PartitionSpec as P


norm_eps = 1e-05
lanes = 128
axes = ("row", "col")
f32 = jnp.float32
bf16 = jnp.bfloat16


def gated_parts(gate):
    sigma = jax.nn.sigmoid(gate)
    return (gate * sigma, sigma * (1.0 + gate * (1.0 - sigma)))


def product(matrix_a, matrix_b):
    return jnp.dot(matrix_a, matrix_b, preferred_element_type=f32)


def product_left(matrix_a, matrix_b):
    return lax.dot_general(matrix_a, matrix_b, (((0,), (0,)), ((), ())), preferred_element_type=f32)


def product_right(matrix_a, matrix_b):
    return lax.dot_general(matrix_a, matrix_b, (((1,), (1,)), ((), ())), preferred_element_type=f32)


def prepare_kernel(n_parts, idx_ref, cot_ref, mask_ref, masked_ref, *refs):
    outs, turned_ref = refs[:-1], refs[-1]
    _, _, n_rows, n_cols, width = cot_ref.shape
    bins = width // 2
    low_t = mask_ref[0, 0].astype(f32).T
    high_t = mask_ref[0, 1].astype(f32).T
    lane = lax.broadcasted_iota(jnp.int32, (n_cols, width), 1)
    for i in range(n_rows):
        low = cot_ref[0, 0, i].astype(f32) * low_t[:, i:i + 1]
        high = cot_ref[0, 1, i].astype(f32) * high_t[:, i:i + 1]
        masked_ref[0, 0, i] = low.astype(bf16)
        masked_ref[0, 1, i] = high.astype(bf16)
        turned_ref[:, i, :] = jnp.where(lane < bins, pltpu.roll(low, bins, 1), high)
    n_cols_piece = n_cols // n_parts
    for turn in range(len(outs) // n_parts):
        @pl.when(pl.program_id(0) == turn)
        def _(turn=turn):
            for part in range(n_parts):
                outs[turn * n_parts + part][...] = turned_ref[
                    part * n_cols_piece:(part + 1) * n_cols_piece
                ].astype(bf16)


def gates(both):
    hidden = both.shape[1] // 2
    up_pre, gate_pre = both[:, :hidden], both[:, hidden:]
    sigma = jnp.tanh(gate_pre * 0.5) * 0.5 + 0.5
    silu = gate_pre * sigma
    return up_pre, sigma, silu, silu * up_pre


def forward_kernel(
    span, n_given, pair_ref, row_ref, col_ref, rpos_ref, cpos_ref, table_ref, up_gate_ref, down_ref, *refs
):
    both_ref, norm_ref, norm_t_ref, inv_ref, out_t_ref = refs[n_given:]
    n_cols, width = pair_ref.shape[1:]
    n_rows = min(pair_ref.shape[0], 1024 // n_cols)
    count = n_rows * n_cols
    for sub in range(pair_ref.shape[0] // n_rows):
        rows = slice(sub * n_rows, (sub + 1) * n_rows)
        flat = slice(sub * count, (sub + 1) * count)
        offset = jnp.clip(rpos_ref[rows][:, None, :] - cpos_ref[...][None, :, :], -span, span) + span
        lane = lax.broadcasted_iota(jnp.int32, offset.shape, 2)
        hot = jnp.where(offset == lane, 1.0, 0.0).astype(bf16).reshape(count, lanes)
        pair_in = pair_ref[rows].astype(f32) + row_ref[rows][:, None, :] + col_ref[...][None, :, :]
        pair_in = pair_in.reshape(count, width) + product(hot, table_ref[...])
        centred = pair_in - jnp.mean(pair_in, axis=-1, keepdims=True)
        inv_std = lax.rsqrt(jnp.mean(centred * centred, axis=-1, keepdims=True) + norm_eps)
        normed_bf = (centred * inv_std).astype(bf16)
        norm_ref[flat] = normed_bf
        norm_t_ref[0, :, flat] = normed_bf.T
        inv_ref[flat] = jnp.broadcast_to(inv_std, (count, width)).astype(bf16)
        both = product(normed_bf, up_gate_ref[...]).astype(bf16)
        both_ref[flat] = both
        hid = gates(both)[3]
        pair_out = (pair_in + product(hid, down_ref[...])).astype(bf16)
        out_t_ref[0, :, flat] = pair_out.T


def backward_kernel(n_pieces, n_given, idx_ref, masked_ref, *refs):
    mirror_refs = refs[:n_pieces]
    (both_ref, norm_ref, norm_t_ref, inv_ref, out_t_ref, bucket_ref,
     head_t_ref, down_t_ref, up_t_ref, gate_t_ref) = refs[n_pieces:n_pieces + 10]
    refs = refs[n_pieces + 10 + n_given:]
    grad_ref, rows_ref, cols_ref, sums_ref, mir_ref, ug_acc, down_acc, head_acc, rel_acc = refs
    piece = pl.program_id(0)
    step = pl.program_id(1)
    first = (piece == 0) & (step == 0)
    last = (piece == pl.num_programs(0) - 1) & (step == pl.num_programs(1) - 1)
    n_cols, width = masked_ref.shape[1:]
    n_rows = min(masked_ref.shape[0], 1024 // n_cols)
    count = n_rows * n_cols
    half = n_cols // 2
    hidden = down_t_ref.shape[1]
    bins = width // 2

    @pl.when(first)
    def _():
        cols_ref[...] = jnp.zeros_like(cols_ref)
        ug_acc[...] = jnp.zeros_like(ug_acc)
        down_acc[...] = jnp.zeros_like(down_acc)
        head_acc[...] = jnp.zeros_like(head_acc)
        rel_acc[...] = jnp.zeros_like(rel_acc)

    for t in range(n_pieces):
        @pl.when(piece == t)
        def _(t=t):
            mir_ref[...] = mirror_refs[t][...]

    for sub in range(masked_ref.shape[0] // n_rows):
        rows = slice(sub * n_rows, (sub + 1) * n_rows)
        flat = slice(sub * count, (sub + 1) * count)
        packed = mir_ref[rows].astype(f32).reshape(n_rows * half, width)
        turned = pltpu.roll(packed, bins, 1).reshape(n_rows, half, width)
        mirrored = jnp.concatenate([turned, packed.reshape(n_rows, half, width)], axis=1)
        lane = lax.broadcasted_iota(jnp.int32, mirrored.shape, 2)
        own = masked_ref[rows].astype(f32)
        head_cot = (own + jnp.where(lane >= bins, mirrored, 0.0)).astype(bf16).reshape(count, width)
        grad_out = product(head_cot, head_t_ref[...])
        grad_out_bf = grad_out.astype(bf16)
        grad_hid = product(grad_out_bf, down_t_ref[...]).astype(bf16)
        up_pre, sigma, silu, hid = gates(both_ref[flat])
        grad_up = grad_hid * silu
        grad_gate = grad_hid * (up_pre * (sigma + silu * (1.0 - sigma)))
        grad_normed = product(grad_up, up_t_ref[...]) + product(grad_gate, gate_t_ref[...])
        normed = norm_ref[flat].astype(f32)
        grad_in = grad_out + inv_ref[flat].astype(f32) * (
            grad_normed
            - jnp.mean(grad_normed, axis=-1, keepdims=True)
            - normed * jnp.mean(grad_normed * normed, axis=-1, keepdims=True)
        )
        grad_tile = grad_in.reshape(n_rows, n_cols, width)
        grad_bf = grad_in.astype(bf16)
        grad_ref[rows] = grad_bf.reshape(n_rows, n_cols, width)
        rows_ref[rows] = jnp.sum(grad_tile, axis=1)
        cols_ref[...] += jnp.sum(grad_tile, axis=0)
        norm_t = norm_t_ref[0, :, flat]
        ug_acc[:, :hidden] += product(norm_t, grad_up)
        ug_acc[:, hidden:] += product(norm_t, grad_gate)
        down_acc[...] += product(grad_out_bf.T, hid)
        head_acc[...] += product(out_t_ref[0, :, flat], head_cot)
        level = lax.broadcasted_iota(jnp.int32, (lanes, count), 0)
        bucket = jnp.broadcast_to(bucket_ref[0, :, flat], (lanes, count))
        rel_acc[...] += product(jnp.where(bucket == level, 1.0, 0.0).astype(bf16), grad_bf)

    @pl.when(last)
    def _():
        n_slabs = hidden // lanes
        for q in range(2 * n_slabs):
            sums_ref[q] = ug_acc[:, q * lanes:(q + 1) * lanes]
        for q in range(n_slabs):
            sums_ref[2 * n_slabs + q] = down_acc[:, q * lanes:(q + 1) * lanes].T
        sums_ref[3 * n_slabs] = head_acc[...]
        sums_ref[3 * n_slabs + 1] = rel_acc[...]


def gather_all(piece, n_dev):
    copies = jnp.broadcast_to(piece[None], (n_dev,) + piece.shape)
    return lax.all_to_all(copies, axes, split_axis=0, concat_axis=0, tiled=True)


def local(
    pair_repr, logit_cotangent, pair_mask, single_repr, token_index, pair_up, pair_gate, pair_down, head_weight,
    rel_table, proj_row, proj_col, single_gate, single_up, single_down,
):
    n_row = lax.axis_size("row")
    n_col = lax.axis_size("col")
    n_dev = n_row * n_col
    fold = n_col // n_row
    row_index = lax.axis_index("row")
    col_index = lax.axis_index("col")
    joint_index = row_index * n_col + col_index
    core = col_index % fold
    tile_rows, tile_cols, width = pair_repr.shape
    bins = width // 2
    half = tile_cols // 2
    strip = single_repr.shape[0]
    tokens = strip * n_dev
    hidden = pair_up.shape[1]
    s_hidden = single_gate.shape[1]
    share = s_hidden // n_dev
    n_rel = rel_table.shape[0]
    span = (n_rel - 1) // 2
    n_groups = 2 if n_row % 2 == 0 else 1
    per_turn = n_row // fold
    piece_rows = tile_cols // per_turn
    block_rows = min(2048 // tile_cols, piece_rows)
    count = block_rows * tile_cols
    n_blocks = tile_rows // block_rows
    n_slabs = hidden // lanes
    n_sums = 3 * n_slabs + 2

    core_arr = core.astype(jnp.int32).reshape(1)
    n_parts = per_turn
    group = 16
    blocks = half // group

    def part_map(s, i, idx):
        return ((idx[0] + s) % fold, 0, i, 0, 0)

    def sent_map(s, i, idx, own=0):
        return (0, jnp.where(s == own, i, jnp.where(s < own, 0, blocks - 1)), 0)

    parted = (fold, 2, half, tile_cols)
    prepared = pl.pallas_call(
        functools.partial(prepare_kernel, n_parts),
        grid_spec=pltpu.PrefetchScalarGridSpec(
            num_scalar_prefetch=1,
            grid=(fold, blocks),
            in_specs=[
                pl.BlockSpec((1, 2, group, tile_cols, width), part_map),
                pl.BlockSpec((1, 2, group, tile_cols), lambda s, i, idx: part_map(s, i, idx)[:4]),
            ],
            out_specs=[pl.BlockSpec((1, 2, group, tile_cols, width), part_map)]
            + [
                pl.BlockSpec((piece_rows, group, width), functools.partial(sent_map, own=t // n_parts))
                for t in range(fold * n_parts)
            ],
            scratch_shapes=[pltpu.VMEM((tile_cols, group, width), f32)],
        ),
        out_shape=[jax.ShapeDtypeStruct(parted + (width,), bf16)]
        + [jax.ShapeDtypeStruct((piece_rows, half, width), bf16)] * (fold * n_parts),
        cost_estimate=pl.CostEstimate(
            flops=tile_rows * tile_cols * width * 4, bytes_accessed=tile_rows * tile_cols * width * 5, transcendentals=0
        ),
        name="mask_and_turn",
    )(core_arr, logit_cotangent.reshape(parted + (width,)), pair_mask.reshape(parted))
    masked = prepared[0].reshape(tile_rows, tile_cols, width)
    sent = prepared[1:]

    def place(r, k, b):
        return r * n_col + k * fold + b

    every = [(r, k, b) for r in range(n_row) for k in range(n_row) for b in range(fold)]
    order = [t for group_no in range(n_groups) for t in range(group_no, n_row, n_groups)]
    pieces = {}
    for t in order:
        spread = [(place(r, k, b), place((r + k + t) % n_row, k, b)) for r, k, b in every]
        pieces[t] = lax.ppermute(sent[t], axes, spread)
    singles = gather_all(single_repr, n_dev).reshape(tokens, -1)

    src = singles.astype(f32)
    inv_rms = lax.rsqrt(jnp.mean(src * src, axis=-1, keepdims=True) + norm_eps)
    s_normed = src * inv_rms
    s_normed_bf = s_normed.astype(bf16)
    s_silu, _ = gated_parts(product(s_normed_bf, single_gate))
    s_hid = (s_silu * product(s_normed_bf, single_up)).astype(bf16)
    updated = (src + product(s_hid, single_down)).astype(bf16)
    row_tokens = lax.dynamic_slice_in_dim(updated, row_index * tile_rows, tile_rows, 0)
    col_tokens = lax.dynamic_slice_in_dim(updated, col_index * tile_cols, tile_cols, 0)
    row_proj = product(row_tokens, proj_row).astype(bf16).astype(f32)
    col_proj = product(col_tokens, proj_col).astype(bf16).astype(f32)

    row_pos = lax.dynamic_slice_in_dim(token_index, row_index * tile_rows, tile_rows, 0)
    col_pos = lax.dynamic_slice_in_dim(token_index, col_index * tile_cols, tile_cols, 0)
    rpos = jnp.broadcast_to(row_pos[:, None], (tile_rows, lanes))
    cpos = jnp.broadcast_to(col_pos[:, None], (tile_cols, lanes))
    bucket = (jnp.clip(row_pos[:, None] - col_pos[None, :], -span, span) + span).reshape(n_blocks, 1, count)
    table = jnp.pad(rel_table, ((0, lanes - n_rel), (0, 0)))
    up_gate = jnp.concatenate([pair_up, pair_gate], axis=1)

    n_pairs = tile_rows * tile_cols
    whole = lambda shape: pl.BlockSpec(shape, lambda *_: (0,) * len(shape))
    flat = lambda cols_, where: pl.BlockSpec((count, cols_), lambda *at: (where(*at), 0))
    lead = lambda shape, where: pl.BlockSpec((1,) + shape, lambda *at: (where(*at), 0, 0))
    tile = lambda where: pl.BlockSpec((block_rows, tile_cols, width), lambda *at: (where(*at), 0, 0))
    some = lambda cols_, where: pl.BlockSpec((block_rows, cols_), lambda *at: (where(*at), 0))
    saved = ()
    n_early = n_blocks * 3 // 8
    for low, high in ((0, n_early), (n_early, n_blocks)):
        part = lambda i, low=low: i + low
        operands = [pair_repr, row_proj, col_proj, rpos, cpos, table, up_gate, pair_down]
        saved = pl.pallas_call(
            functools.partial(forward_kernel, span, len(saved)),
            grid=(high - low,),
            in_specs=[
                tile(part), some(width, part), whole((tile_cols, width)), some(lanes, part), whole((tile_cols, lanes)),
                whole(table.shape), whole(up_gate.shape), whole(pair_down.shape),
            ]
            + [pl.BlockSpec(memory_space=pl.ANY)] * len(saved),
            out_specs=[
                flat(2 * hidden, part), flat(width, part), lead((width, count), part), flat(width, part),
                lead((width, count), part),
            ],
            out_shape=[
                jax.ShapeDtypeStruct((n_pairs, 2 * hidden), bf16),
                jax.ShapeDtypeStruct((n_pairs, width), bf16),
                jax.ShapeDtypeStruct((n_blocks, width, count), bf16),
                jax.ShapeDtypeStruct((n_pairs, width), bf16),
                jax.ShapeDtypeStruct((n_blocks, width, count), bf16),
            ],
            input_output_aliases={len(operands) + i: i for i in range(len(saved))},
            cost_estimate=pl.CostEstimate(
                flops=2 * n_pairs * width * (3 * hidden + lanes) * (high - low) // n_blocks,
                bytes_accessed=n_pairs * (4 * hidden + 10 * width) * (high - low) // n_blocks,
                transcendentals=n_pairs * hidden * (high - low) // n_blocks,
            ),
            name="pair_forward",
        )(*operands, *saved)
        if low == 0:
            held, inv_held = lax.optimization_barrier((pieces, saved[3]))
            saved = list(saved[:3]) + [inv_held] + list(saved[4:])
            for t in order:
                s = t // per_turn
                onward = [
                    (place((r + k + t) % n_row, k, b), place(k, r, (b + s) % fold)) for r, k, b in every
                ]
                pieces[t] = lax.ppermute(held[t], axes, onward)

    head_t = head_weight.T
    down_t = pair_down.T
    up_t = pair_up.T
    gate_t = pair_gate.T
    steps = piece_rows // block_rows
    n_pieces = n_row // n_groups
    given = ()
    sums, cols = 0.0, 0.0
    for group_no in range(n_groups):
        def block_of(p, j, idx, group_no=group_no):
            t = p * n_groups + group_no
            strip_no = (idx[0] + fold - t // per_turn) % fold
            return strip_no * (tile_cols // block_rows) + (t % per_turn) * steps + j

        def mirror_map(p, j, idx, own=0):
            return (jnp.where(p == own, j, jnp.where(p < own, 0, steps - 1)), 0, 0)

        in_specs = (
            [tile(block_of)]
            + [
                pl.BlockSpec((block_rows, half, width), functools.partial(mirror_map, own=p))
                for p in range(n_pieces)
            ]
            + [flat(2 * hidden, block_of), flat(width, block_of), lead((width, count), block_of),
               flat(width, block_of), lead((width, count), block_of), lead((1, count), block_of),
               whole(head_t.shape), whole(down_t.shape), whole(up_t.shape), whole(gate_t.shape)]
            + [pl.BlockSpec(memory_space=pl.ANY)] * len(given)
        )
        operands = [masked] + [pieces[p * n_groups + group_no] for p in range(n_pieces)] + list(saved) + [
            bucket, head_t, down_t, up_t, gate_t] + list(given)
        first_given = 1 + len(operands) - len(given)
        pair_grad, row_part, col_part, sum_part = pl.pallas_call(
            functools.partial(backward_kernel, n_pieces, len(given)),
            grid_spec=pltpu.PrefetchScalarGridSpec(
                num_scalar_prefetch=1,
                grid=(n_pieces, steps),
                in_specs=in_specs,
                out_specs=[
                    tile(block_of), some(width, block_of), whole((tile_cols, width)), whole((n_sums, lanes, lanes)),
                ],
                scratch_shapes=[
                    pltpu.VMEM((block_rows, half, width), bf16),
                    pltpu.VMEM((width, 2 * hidden), f32),
                    pltpu.VMEM((width, hidden), f32),
                    pltpu.VMEM((width, lanes), f32),
                    pltpu.VMEM((lanes, width), f32),
                ],
            ),
            out_shape=[
                jax.ShapeDtypeStruct(pair_repr.shape, bf16),
                jax.ShapeDtypeStruct((tile_rows, width), f32),
                jax.ShapeDtypeStruct((tile_cols, width), f32),
                jax.ShapeDtypeStruct((n_sums, lanes, lanes), f32),
            ],
            input_output_aliases={first_given + i: i for i in range(len(given))},
            cost_estimate=pl.CostEstimate(
                flops=2 * n_pairs * width * (6 * hidden + 3 * lanes) // n_groups,
                bytes_accessed=n_pairs * (4 * hidden + 13 * width) // n_groups,
                transcendentals=n_pairs * hidden // n_groups,
            ),
            name="pair_backward",
        )(core_arr, *operands)
        given = (pair_grad, row_part)
        sums = sums + sum_part
        cols = cols + col_part

    sum_rows = n_sums * lanes // n_dev

    def spread_out(part):
        size = part.size // n_dev
        narrow = min(size, lanes)
        return jnp.pad(part.reshape(n_dev, size // narrow, narrow), ((0, 0), (0, 0), (0, lanes - narrow)))

    row_sent, col_sent = spread_out(row_part), spread_out(cols)
    row_len, col_len = row_sent.shape[1], col_sent.shape[1]
    outgoing = jnp.concatenate([sums.reshape(n_dev, sum_rows, lanes), row_sent, col_sent], axis=1).astype(bf16)
    arrived = lax.all_to_all(outgoing, axes, split_axis=0, concat_axis=0, tiled=True).astype(f32)
    row_own = jnp.sum(arrived[:, sum_rows:sum_rows + row_len].reshape(n_row, n_col, row_len, lanes), axis=1)
    col_own = jnp.sum(arrived[:, sum_rows + row_len:].reshape(n_row, n_col, col_len, lanes), axis=0)
    totals = jnp.concatenate(
        [row_own.reshape(n_row * row_len, lanes), col_own.reshape(n_col * col_len, lanes)], axis=0
    ).astype(bf16)
    grad_scale = 1.0 / tokens
    own_sums = (jnp.sum(arrived[:, :sum_rows], axis=0) * grad_scale).astype(bf16)
    totals_all = gather_all(totals, n_dev)
    own_sums, totals_all = lax.optimization_barrier((own_sums, totals_all))
    slabs = gather_all(own_sums, n_dev).reshape(n_sums, lanes, lanes).astype(f32)

    def tokens_of(held, n_strips, length):
        used = tokens * width // (n_strips * n_dev * length)
        return held.reshape(n_dev, n_strips, length, lanes)[..., :used].transpose(1, 0, 2, 3).reshape(tokens, width)

    row_bf = tokens_of(totals_all[:, :n_row * row_len], n_row, row_len)
    col_bf = tokens_of(totals_all[:, n_row * row_len:], n_col, col_len)

    single_cot = product_right(row_bf, proj_row) + product_right(col_bf, proj_col)
    cot_bf = single_cot.astype(bf16)
    prow_sum = product_left(updated, row_bf)
    pcol_sum = product_left(updated, col_bf)
    gate_cols = lax.dynamic_slice_in_dim(single_gate, joint_index * share, share, 1)
    up_cols = lax.dynamic_slice_in_dim(single_up, joint_index * share, share, 1)
    down_rows = lax.dynamic_slice_in_dim(single_down, joint_index * share, share, 0)
    own_up = product(s_normed_bf, up_cols)
    own_silu, own_slope = gated_parts(product(s_normed_bf, gate_cols))
    own_hid = (own_silu * own_up).astype(bf16)
    own_grad_hid = product_right(cot_bf, down_rows)
    own_grad_up = (own_grad_hid * own_silu).astype(bf16)
    own_grad_gate = (own_grad_hid * own_up * own_slope).astype(bf16)
    gate_sum = product_left(s_normed_bf, own_grad_gate)
    up_sum = product_left(s_normed_bf, own_grad_up)
    down_sum = product_left(own_hid, cot_bf)

    mine = lambda whole_: lax.dynamic_slice_in_dim(whole_, joint_index * strip, strip, 0)
    my_src = single_repr.astype(f32)
    my_inv = lax.rsqrt(jnp.mean(my_src * my_src, axis=-1, keepdims=True) + norm_eps)
    my_normed = my_src * my_inv
    my_normed_bf = my_normed.astype(bf16)
    my_up = product(my_normed_bf, single_up)
    my_silu, my_slope = gated_parts(product(my_normed_bf, single_gate))
    my_cot = mine(single_cot)
    my_grad_hid = product_right(my_cot.astype(bf16), single_down)
    my_grad_up = (my_grad_hid * my_silu).astype(bf16)
    my_grad_gate = (my_grad_hid * my_up * my_slope).astype(bf16)
    my_grad_normed = product_right(my_grad_gate, single_gate) + product_right(my_grad_up, single_up)
    single_grad = my_cot + my_inv * (
        my_grad_normed - my_normed * jnp.mean(my_grad_normed * my_normed, axis=-1, keepdims=True)
    )

    def wide(first):
        return slabs[first:first + n_slabs].transpose(1, 0, 2).reshape(width, hidden)

    return (
        pair_grad,
        single_grad.astype(bf16),
        wide(0),
        wide(n_slabs),
        slabs[2 * n_slabs:3 * n_slabs].reshape(hidden, width),
        slabs[3 * n_slabs],
        slabs[3 * n_slabs + 1][:n_rel],
        prow_sum * grad_scale,
        pcol_sum * grad_scale,
        gate_sum * grad_scale,
        up_sum * grad_scale,
        down_sum * grad_scale,
    )


def solution(mesh):
    placed = (
        P("row", "col", None),
        P("row", "col", None),
        P("row", "col"),
        P(("row", "col"), None),
    ) + (P(),) * 11
    return jax.shard_map(
        local,
        mesh=mesh,
        in_specs=placed,
        out_specs=(P("row", "col", None), P(("row", "col"), None))
        + (P(),) * 7
        + (P(None, ("row", "col")), P(None, ("row", "col")), P(("row", "col"), None)),
        check_vma=False,
    )
```

```python
import functools

import jax
import jax.numpy as jnp
from jax import lax
from jax.experimental import pallas as pl
from jax.experimental.pallas import tpu as pltpu
from jax.sharding import PartitionSpec as P


norm_eps = 1e-05
lanes = 128
axes = ("row", "col")
f32 = jnp.float32
bf16 = jnp.bfloat16


def gated_parts(gate):
    sigma = jax.nn.sigmoid(gate)
    return (gate * sigma, sigma * (1.0 + gate * (1.0 - sigma)))


def product(matrix_a, matrix_b):
    return jnp.dot(matrix_a, matrix_b, preferred_element_type=f32)


def product_left(matrix_a, matrix_b):
    return lax.dot_general(matrix_a, matrix_b, (((0,), (0,)), ((), ())), preferred_element_type=f32)


def product_right(matrix_a, matrix_b):
    return lax.dot_general(matrix_a, matrix_b, (((1,), (1,)), ((), ())), preferred_element_type=f32)


def prepare_kernel(n_parts, idx_ref, cot_ref, mask_ref, *refs):
    outs, turned_ref = refs[:-1], refs[-1]
    _, _, n_rows, n_cols, width = cot_ref.shape
    bins = width // 2
    low_t = mask_ref[0, 0].astype(f32).T
    high_t = mask_ref[0, 1].astype(f32).T
    lane = lax.broadcasted_iota(jnp.int32, (n_cols, width), 1)
    for i in range(n_rows):
        low = pltpu.roll(cot_ref[0, 0, i].astype(f32), bins, 1) * low_t[:, i:i + 1]
        high = cot_ref[0, 1, i].astype(f32) * high_t[:, i:i + 1]
        turned_ref[:, i, :] = jnp.where(lane < bins, low, high)
    n_cols_piece = n_cols // n_parts
    for turn in range(len(outs) // n_parts):
        @pl.when(pl.program_id(0) == turn)
        def _(turn=turn):
            for part in range(n_parts):
                outs[turn * n_parts + part][...] = turned_ref[
                    part * n_cols_piece:(part + 1) * n_cols_piece
                ].astype(bf16)


def gates(both):
    hidden = both.shape[1] // 2
    up_pre, gate_pre = both[:, :hidden], both[:, hidden:]
    sigma = jnp.tanh(gate_pre * 0.5) * 0.5 + 0.5
    silu = gate_pre * sigma
    return up_pre, sigma, silu, silu * up_pre


def forward_kernel(
    span, n_given, pair_ref, row_ref, col_ref, rpos_ref, cpos_ref, table_ref, up_gate_ref, down_ref, *refs
):
    both_ref, norm_ref, norm_t_ref, inv_ref, out_t_ref = refs[n_given:]
    n_cols, width = pair_ref.shape[1:]
    n_rows = min(pair_ref.shape[0], 1024 // n_cols)
    count = n_rows * n_cols
    for sub in range(pair_ref.shape[0] // n_rows):
        rows = slice(sub * n_rows, (sub + 1) * n_rows)
        flat = slice(sub * count, (sub + 1) * count)
        offset = jnp.clip(rpos_ref[rows][:, None, :] - cpos_ref[...][None, :, :], -span, span) + span
        lane = lax.broadcasted_iota(jnp.int32, offset.shape, 2)
        hot = jnp.where(offset == lane, 1.0, 0.0).astype(bf16).reshape(count, lanes)
        pair_in = pair_ref[rows].astype(f32) + row_ref[rows][:, None, :] + col_ref[...][None, :, :]
        pair_in = pair_in.reshape(count, width) + product(hot, table_ref[...])
        centred = pair_in - jnp.mean(pair_in, axis=-1, keepdims=True)
        inv_std = lax.rsqrt(jnp.mean(centred * centred, axis=-1, keepdims=True) + norm_eps)
        normed_bf = (centred * inv_std).astype(bf16)
        norm_ref[flat] = normed_bf
        norm_t_ref[0, :, flat] = normed_bf.T
        inv_ref[flat] = jnp.broadcast_to(inv_std, (count, width)).astype(bf16)
        both = product(normed_bf, up_gate_ref[...]).astype(bf16)
        both_ref[flat] = both
        hid = gates(both)[3]
        pair_out = (pair_in + product(hid, down_ref[...])).astype(bf16)
        out_t_ref[0, :, flat] = pair_out.T


def backward_kernel(n_pieces, n_given, idx_ref, cot_ref, mask_ref, *refs):
    mirror_refs = refs[:n_pieces]
    (both_ref, norm_ref, norm_t_ref, inv_ref, out_t_ref, bucket_ref,
     head_t_ref, down_t_ref, up_t_ref, gate_t_ref) = refs[n_pieces:n_pieces + 10]
    refs = refs[n_pieces + 10 + n_given:]
    grad_ref, rows_ref, cols_ref, sums_ref, mir_ref, ug_acc, down_acc, head_acc, rel_acc = refs
    piece = pl.program_id(0)
    step = pl.program_id(1)
    first = (piece == 0) & (step == 0)
    last = (piece == pl.num_programs(0) - 1) & (step == pl.num_programs(1) - 1)
    n_cols, width = cot_ref.shape[1:]
    n_rows = min(cot_ref.shape[0], 1024 // n_cols)
    count = n_rows * n_cols
    half = n_cols // 2
    hidden = down_t_ref.shape[1]
    bins = width // 2

    @pl.when(first)
    def _():
        cols_ref[...] = jnp.zeros_like(cols_ref)
        ug_acc[...] = jnp.zeros_like(ug_acc)
        down_acc[...] = jnp.zeros_like(down_acc)
        head_acc[...] = jnp.zeros_like(head_acc)
        rel_acc[...] = jnp.zeros_like(rel_acc)

    for t in range(n_pieces):
        @pl.when(piece == t)
        def _(t=t):
            mir_ref[...] = mirror_refs[t][...]

    for sub in range(cot_ref.shape[0] // n_rows):
        rows = slice(sub * n_rows, (sub + 1) * n_rows)
        flat = slice(sub * count, (sub + 1) * count)
        packed = mir_ref[rows].astype(f32).reshape(n_rows * half, width)
        turned = pltpu.roll(packed, bins, 1).reshape(n_rows, half, width)
        mirrored = jnp.concatenate([turned, packed.reshape(n_rows, half, width)], axis=1)
        lane = lax.broadcasted_iota(jnp.int32, mirrored.shape, 2)
        mask_t = mask_ref[rows].astype(f32).T
        own = jnp.stack([cot_ref[sub * n_rows + i].astype(f32) * mask_t[:, i:i + 1] for i in range(n_rows)], axis=0)
        head_cot = (own + jnp.where(lane >= bins, mirrored, 0.0)).astype(bf16).reshape(count, width)
        grad_out = product(head_cot, head_t_ref[...])
        grad_out_bf = grad_out.astype(bf16)
        grad_hid = product(grad_out_bf, down_t_ref[...]).astype(bf16)
        up_pre, sigma, silu, hid = gates(both_ref[flat])
        grad_up = grad_hid * silu
        grad_gate = grad_hid * (up_pre * (sigma + silu * (1.0 - sigma)))
        grad_normed = product(grad_up, up_t_ref[...]) + product(grad_gate, gate_t_ref[...])
        normed = norm_ref[flat].astype(f32)
        grad_in = grad_out + inv_ref[flat].astype(f32) * (
            grad_normed
            - jnp.mean(grad_normed, axis=-1, keepdims=True)
            - normed * jnp.mean(grad_normed * normed, axis=-1, keepdims=True)
        )
        grad_tile = grad_in.reshape(n_rows, n_cols, width)
        grad_bf = grad_in.astype(bf16)
        grad_ref[rows] = grad_bf.reshape(n_rows, n_cols, width)
        rows_ref[rows] = jnp.sum(grad_tile, axis=1)
        cols_ref[...] += jnp.sum(grad_tile, axis=0)
        norm_t = norm_t_ref[0, :, flat]
        ug_acc[:, :hidden] += product(norm_t, grad_up)
        ug_acc[:, hidden:] += product(norm_t, grad_gate)
        down_acc[...] += product(grad_out_bf.T, hid)
        head_acc[...] += product(out_t_ref[0, :, flat], head_cot)
        level = lax.broadcasted_iota(jnp.int32, (lanes, count), 0)
        bucket = jnp.broadcast_to(bucket_ref[0, :, flat], (lanes, count))
        rel_acc[...] += product(jnp.where(bucket == level, 1.0, 0.0).astype(bf16), grad_bf)

    @pl.when(last)
    def _():
        n_slabs = hidden // lanes
        for q in range(2 * n_slabs):
            sums_ref[q] = ug_acc[:, q * lanes:(q + 1) * lanes]
        for q in range(n_slabs):
            sums_ref[2 * n_slabs + q] = down_acc[:, q * lanes:(q + 1) * lanes].T
        sums_ref[3 * n_slabs] = head_acc[...]
        sums_ref[3 * n_slabs + 1] = rel_acc[...]


def transition(tokens_in, single_gate, single_up, single_down):
    src = tokens_in.astype(f32)
    inv_rms = lax.rsqrt(jnp.mean(src * src, axis=-1, keepdims=True) + norm_eps)
    normed_bf = (src * inv_rms).astype(bf16)
    silu, _ = gated_parts(product(normed_bf, single_gate))
    hid = (silu * product(normed_bf, single_up)).astype(bf16)
    updated = (src + product(hid, single_down)).astype(bf16)
    return normed_bf, hid, updated


def gather_all(piece, n_dev):
    copies = jnp.broadcast_to(piece[None], (n_dev,) + piece.shape)
    return lax.all_to_all(copies, axes, split_axis=0, concat_axis=0, tiled=True)


def local(
    pair_repr, logit_cotangent, pair_mask, single_repr, token_index, pair_up, pair_gate, pair_down, head_weight,
    rel_table, proj_row, proj_col, single_gate, single_up, single_down,
):
    n_row = lax.axis_size("row")
    n_col = lax.axis_size("col")
    n_dev = n_row * n_col
    fold = n_col // n_row
    row_index = lax.axis_index("row")
    col_index = lax.axis_index("col")
    joint_index = row_index * n_col + col_index
    core = col_index % fold
    tile_rows, tile_cols, width = pair_repr.shape
    half = tile_cols // 2
    strip = single_repr.shape[0]
    tokens = strip * n_dev
    hidden = pair_up.shape[1]
    s_hidden = single_gate.shape[1]
    share = s_hidden // n_dev
    n_rel = rel_table.shape[0]
    span = (n_rel - 1) // 2
    n_groups = 2 if n_row % 2 == 0 else 1
    per_turn = n_row // fold
    piece_rows = tile_cols // per_turn
    block_rows = min(2048 // tile_cols, piece_rows)
    count = block_rows * tile_cols
    n_blocks = tile_rows // block_rows
    n_slabs = hidden // lanes
    n_sums = 3 * n_slabs + 2

    core_arr = core.astype(jnp.int32).reshape(1)
    n_parts = per_turn
    group = 16
    blocks = half // group

    def part_map(s, i, idx):
        return ((idx[0] + s) % fold, 0, i, 0, 0)

    def sent_map(s, i, idx, own=0):
        return (0, jnp.where(s == own, i, jnp.where(s < own, 0, blocks - 1)), 0)

    parted = (fold, 2, half, tile_cols)
    prepared = pl.pallas_call(
        functools.partial(prepare_kernel, n_parts),
        grid_spec=pltpu.PrefetchScalarGridSpec(
            num_scalar_prefetch=1,
            grid=(fold, blocks),
            in_specs=[
                pl.BlockSpec((1, 2, group, tile_cols, width), part_map),
                pl.BlockSpec((1, 2, group, tile_cols), lambda s, i, idx: part_map(s, i, idx)[:4]),
            ],
            out_specs=[
                pl.BlockSpec((piece_rows, group, width), functools.partial(sent_map, own=t // n_parts))
                for t in range(fold * n_parts)
            ],
            scratch_shapes=[pltpu.VMEM((tile_cols, group, width), f32)],
        ),
        out_shape=[jax.ShapeDtypeStruct((piece_rows, half, width), bf16)] * (fold * n_parts),
        cost_estimate=pl.CostEstimate(
            flops=tile_rows * tile_cols * width * 4, bytes_accessed=tile_rows * tile_cols * width * 3, transcendentals=0
        ),
        name="mask_and_turn",
    )(core_arr, logit_cotangent.reshape(parted + (width,)), pair_mask.reshape(parted))
    sent = prepared

    def place(r, k, b):
        return r * n_col + k * fold + b

    every = [(r, k, b) for r in range(n_row) for k in range(n_row) for b in range(fold)]

    def onward(t):
        s = t // per_turn
        return [(place((r + k + t) % n_row, k, b), place(k, r, (b + s) % fold)) for r, k, b in every]

    order = [t for group_no in range(n_groups) for t in range(group_no, n_row, n_groups)]
    pieces = {}
    for t in order:
        spread = [(place(r, k, b), place((r + k + t) % n_row, k, b)) for r, k, b in every]
        pieces[t] = lax.ppermute(sent[t], axes, spread)
    singles = gather_all(single_repr, n_dev).reshape(tokens, -1)

    row_pos = lax.dynamic_slice_in_dim(token_index, row_index * tile_rows, tile_rows, 0)
    col_pos = lax.dynamic_slice_in_dim(token_index, col_index * tile_cols, tile_cols, 0)
    rpos = jnp.broadcast_to(row_pos[:, None], (tile_rows, lanes))
    cpos = jnp.broadcast_to(col_pos[:, None], (tile_cols, lanes))
    bucket = (jnp.clip(row_pos[:, None] - col_pos[None, :], -span, span) + span).reshape(n_blocks, 1, count)
    table = jnp.pad(rel_table, ((0, lanes - n_rel), (0, 0)))
    up_gate = jnp.concatenate([pair_up, pair_gate], axis=1)

    singles, rpos, cpos, bucket, table, up_gate = lax.optimization_barrier(
        (singles, rpos, cpos, bucket, table, up_gate)
    )
    near = jnp.concatenate(
        [
            lax.dynamic_slice_in_dim(singles, row_index * tile_rows, tile_rows, 0),
            lax.dynamic_slice_in_dim(singles, col_index * tile_cols, tile_cols, 0),
        ],
        axis=0,
    )
    near_updated = transition(near, single_gate, single_up, single_down)[2]
    row_proj = product(near_updated[:tile_rows], proj_row).astype(bf16).astype(f32)
    col_proj = product(near_updated[tile_rows:], proj_col).astype(bf16).astype(f32)

    n_pairs = tile_rows * tile_cols
    whole = lambda shape: pl.BlockSpec(shape, lambda *_: (0,) * len(shape))
    flat = lambda cols_, where: pl.BlockSpec((count, cols_), lambda *at: (where(*at), 0))
    lead = lambda shape, where: pl.BlockSpec((1,) + shape, lambda *at: (where(*at), 0, 0))
    tile = lambda where: pl.BlockSpec((block_rows, tile_cols, width), lambda *at: (where(*at), 0, 0))
    some = lambda cols_, where: pl.BlockSpec((block_rows, cols_), lambda *at: (where(*at), 0))
    saved = ()
    n_early = n_blocks * 3 // 8
    for low, high in ((0, n_early), (n_early, n_blocks)):
        part = lambda i, low=low: i + low
        operands = [pair_repr, row_proj, col_proj, rpos, cpos, table, up_gate, pair_down]
        saved = pl.pallas_call(
            functools.partial(forward_kernel, span, len(saved)),
            grid=(high - low,),
            in_specs=[
                tile(part), some(width, part), whole((tile_cols, width)), some(lanes, part), whole((tile_cols, lanes)),
                whole(table.shape), whole(up_gate.shape), whole(pair_down.shape),
            ]
            + [pl.BlockSpec(memory_space=pl.ANY)] * len(saved),
            out_specs=[
                flat(2 * hidden, part), flat(width, part), lead((width, count), part), flat(width, part),
                lead((width, count), part),
            ],
            out_shape=[
                jax.ShapeDtypeStruct((n_pairs, 2 * hidden), bf16),
                jax.ShapeDtypeStruct((n_pairs, width), bf16),
                jax.ShapeDtypeStruct((n_blocks, width, count), bf16),
                jax.ShapeDtypeStruct((n_pairs, width), bf16),
                jax.ShapeDtypeStruct((n_blocks, width, count), bf16),
            ],
            input_output_aliases={len(operands) + i: i for i in range(len(saved))},
            cost_estimate=pl.CostEstimate(
                flops=2 * n_pairs * width * (3 * hidden + lanes) * (high - low) // n_blocks,
                bytes_accessed=n_pairs * (4 * hidden + 10 * width) * (high - low) // n_blocks,
                transcendentals=n_pairs * hidden * (high - low) // n_blocks,
            ),
            name="pair_forward",
        )(*operands, *saved)
        if low == 0:
            held, inv_held = lax.optimization_barrier((pieces, saved[3]))
            saved = list(saved[:3]) + [inv_held] + list(saved[4:])
            for t in range(0, n_row, n_groups):
                pieces[t] = lax.ppermute(held[t], axes, onward(t))
    late = [t for t in range(n_row) if t % n_groups]
    if late:
        held, inv_held = lax.optimization_barrier((held, saved[3]))
        saved = list(saved[:3]) + [inv_held] + list(saved[4:])
        for t in late:
            pieces[t] = lax.ppermute(held[t], axes, onward(t))

    head_t = head_weight.T
    down_t = pair_down.T
    up_t = pair_up.T
    gate_t = pair_gate.T
    steps = piece_rows // block_rows
    n_pieces = n_row // n_groups
    given = ()
    sums, cols = 0.0, 0.0
    for group_no in range(n_groups):
        def block_of(p, j, idx, group_no=group_no):
            t = p * n_groups + group_no
            strip_no = (idx[0] + fold - t // per_turn) % fold
            return strip_no * (tile_cols // block_rows) + (t % per_turn) * steps + j

        def mirror_map(p, j, idx, own=0):
            return (jnp.where(p == own, j, jnp.where(p < own, 0, steps - 1)), 0, 0)

        in_specs = (
            [tile(block_of), some(tile_cols, block_of)]
            + [
                pl.BlockSpec((block_rows, half, width), functools.partial(mirror_map, own=p))
                for p in range(n_pieces)
            ]
            + [flat(2 * hidden, block_of), flat(width, block_of), lead((width, count), block_of),
               flat(width, block_of), lead((width, count), block_of), lead((1, count), block_of),
               whole(head_t.shape), whole(down_t.shape), whole(up_t.shape), whole(gate_t.shape)]
            + [pl.BlockSpec(memory_space=pl.ANY)] * len(given)
        )
        operands = [logit_cotangent, pair_mask] + [pieces[p * n_groups + group_no] for p in range(n_pieces)] + list(saved) + [
            bucket, head_t, down_t, up_t, gate_t] + list(given)
        first_given = 1 + len(operands) - len(given)
        pair_grad, row_part, col_part, sum_part = pl.pallas_call(
            functools.partial(backward_kernel, n_pieces, len(given)),
            grid_spec=pltpu.PrefetchScalarGridSpec(
                num_scalar_prefetch=1,
                grid=(n_pieces, steps),
                in_specs=in_specs,
                out_specs=[
                    tile(block_of), some(width, block_of), whole((tile_cols, width)), whole((n_sums, lanes, lanes)),
                ],
                scratch_shapes=[
                    pltpu.VMEM((block_rows, half, width), bf16),
                    pltpu.VMEM((width, 2 * hidden), f32),
                    pltpu.VMEM((width, hidden), f32),
                    pltpu.VMEM((width, lanes), f32),
                    pltpu.VMEM((lanes, width), f32),
                ],
            ),
            out_shape=[
                jax.ShapeDtypeStruct(pair_repr.shape, bf16),
                jax.ShapeDtypeStruct((tile_rows, width), f32),
                jax.ShapeDtypeStruct((tile_cols, width), f32),
                jax.ShapeDtypeStruct((n_sums, lanes, lanes), f32),
            ],
            input_output_aliases={first_given + i: i for i in range(len(given))},
            cost_estimate=pl.CostEstimate(
                flops=2 * n_pairs * width * (6 * hidden + 3 * lanes) // n_groups,
                bytes_accessed=n_pairs * (4 * hidden + 13 * width) // n_groups,
                transcendentals=n_pairs * hidden // n_groups,
            ),
            name="pair_backward",
        )(core_arr, *operands)
        given = (pair_grad, row_part)
        sums = sums + sum_part
        cols = cols + col_part

    sum_rows = n_sums * lanes // n_dev

    def spread_out(part):
        size = part.size // n_dev
        narrow = min(size, lanes)
        return jnp.pad(part.reshape(n_dev, size // narrow, narrow), ((0, 0), (0, 0), (0, lanes - narrow)))

    row_sent, col_sent = spread_out(row_part), spread_out(cols)
    row_len, col_len = row_sent.shape[1], col_sent.shape[1]
    outgoing = jnp.concatenate([sums.reshape(n_dev, sum_rows, lanes), row_sent, col_sent], axis=1).astype(bf16)
    outgoing, singles = lax.optimization_barrier((outgoing, singles))
    s_normed_bf, _, updated = transition(singles, single_gate, single_up, single_down)
    arrived = lax.all_to_all(outgoing, axes, split_axis=0, concat_axis=0, tiled=True).astype(f32)
    row_own = jnp.sum(arrived[:, sum_rows:sum_rows + row_len].reshape(n_row, n_col, row_len, lanes), axis=1)
    col_own = jnp.sum(arrived[:, sum_rows + row_len:].reshape(n_row, n_col, col_len, lanes), axis=0)
    totals = jnp.concatenate(
        [row_own.reshape(n_row * row_len, lanes), col_own.reshape(n_col * col_len, lanes)], axis=0
    ).astype(bf16)
    grad_scale = 1.0 / tokens
    own_sums = (jnp.sum(arrived[:, :sum_rows], axis=0) * grad_scale).astype(bf16)
    totals_all = gather_all(totals, n_dev)
    own_sums, totals_all = lax.optimization_barrier((own_sums, totals_all))
    shared = gather_all(own_sums, n_dev)
    slabs = shared.reshape(n_sums, lanes, lanes).astype(f32)

    def tokens_of(held, n_strips, length):
        used = tokens * width // (n_strips * n_dev * length)
        return held.reshape(n_dev, n_strips, length, lanes)[..., :used].transpose(1, 0, 2, 3).reshape(tokens, width)

    row_bf = tokens_of(totals_all[:, :n_row * row_len], n_row, row_len)
    col_bf = tokens_of(totals_all[:, n_row * row_len:], n_col, col_len)

    single_cot = product_right(row_bf, proj_row) + product_right(col_bf, proj_col)
    cot_bf = single_cot.astype(bf16)
    prow_sum = product_left(updated, row_bf)
    pcol_sum = product_left(updated, col_bf)
    gate_cols = lax.dynamic_slice_in_dim(single_gate, joint_index * share, share, 1)
    up_cols = lax.dynamic_slice_in_dim(single_up, joint_index * share, share, 1)
    down_rows = lax.dynamic_slice_in_dim(single_down, joint_index * share, share, 0)
    own_up = product(s_normed_bf, up_cols)
    own_silu, own_slope = gated_parts(product(s_normed_bf, gate_cols))
    own_hid = (own_silu * own_up).astype(bf16)
    own_grad_hid = product_right(cot_bf, down_rows)
    own_grad_up = (own_grad_hid * own_silu).astype(bf16)
    own_grad_gate = (own_grad_hid * own_up * own_slope).astype(bf16)
    gate_sum = product_left(s_normed_bf, own_grad_gate)
    up_sum = product_left(s_normed_bf, own_grad_up)
    down_sum = product_left(own_hid, cot_bf)

    mine = lambda whole_: lax.dynamic_slice_in_dim(whole_, joint_index * strip, strip, 0)
    my_src = single_repr.astype(f32)
    my_inv = lax.rsqrt(jnp.mean(my_src * my_src, axis=-1, keepdims=True) + norm_eps)
    my_normed = my_src * my_inv
    my_normed_bf = my_normed.astype(bf16)
    my_up = product(my_normed_bf, single_up)
    my_silu, my_slope = gated_parts(product(my_normed_bf, single_gate))
    my_cot = mine(single_cot)
    my_grad_hid = product_right(my_cot.astype(bf16), single_down)
    my_grad_up = (my_grad_hid * my_silu).astype(bf16)
    my_grad_gate = (my_grad_hid * my_up * my_slope).astype(bf16)
    my_grad_normed = product_right(my_grad_gate, single_gate) + product_right(my_grad_up, single_up)
    single_grad = my_cot + my_inv * (
        my_grad_normed - my_normed * jnp.mean(my_grad_normed * my_normed, axis=-1, keepdims=True)
    )

    def wide(first):
        return slabs[first:first + n_slabs].transpose(1, 0, 2).reshape(width, hidden)

    return (
        pair_grad,
        single_grad.astype(bf16),
        wide(0),
        wide(n_slabs),
        slabs[2 * n_slabs:3 * n_slabs].reshape(hidden, width),
        slabs[3 * n_slabs],
        slabs[3 * n_slabs + 1][:n_rel],
        prow_sum * grad_scale,
        pcol_sum * grad_scale,
        gate_sum * grad_scale,
        up_sum * grad_scale,
        down_sum * grad_scale,
    )


def solution(mesh):
    placed = (
        P("row", "col", None),
        P("row", "col", None),
        P("row", "col"),
        P(("row", "col"), None),
    ) + (P(),) * 11
    return jax.shard_map(
        local,
        mesh=mesh,
        in_specs=placed,
        out_specs=(P("row", "col", None), P(("row", "col"), None))
        + (P(),) * 7
        + (P(None, ("row", "col")), P(None, ("row", "col")), P(("row", "col"), None)),
        check_vma=False,
    )
```

```python
import functools

import jax
import jax.numpy as jnp
from jax import lax
from jax.experimental import pallas as pl
from jax.experimental.pallas import tpu as pltpu
from jax.sharding import PartitionSpec as P


norm_eps = 1e-05
lanes = 128
axes = ("row", "col")
f32 = jnp.float32
bf16 = jnp.bfloat16


def gated_parts(gate):
    sigma = jax.nn.sigmoid(gate)
    return (gate * sigma, sigma * (1.0 + gate * (1.0 - sigma)))


def product(matrix_a, matrix_b):
    return jnp.dot(matrix_a, matrix_b, preferred_element_type=f32)


def product_left(matrix_a, matrix_b):
    return lax.dot_general(matrix_a, matrix_b, (((0,), (0,)), ((), ())), preferred_element_type=f32)


def product_right(matrix_a, matrix_b):
    return lax.dot_general(matrix_a, matrix_b, (((1,), (1,)), ((), ())), preferred_element_type=f32)


def prepare_kernel(n_parts, idx_ref, cot_ref, mask_ref, *refs):
    outs, turned_ref = refs[:-1], refs[-1]
    _, _, n_rows, n_cols, width = cot_ref.shape
    bins = width // 2
    low_t = mask_ref[0, 0].astype(f32).T
    high_t = mask_ref[0, 1].astype(f32).T
    lane = lax.broadcasted_iota(jnp.int32, (n_cols, width), 1)
    for i in range(n_rows):
        low = pltpu.roll(cot_ref[0, 0, i].astype(f32), bins, 1) * low_t[:, i:i + 1]
        high = cot_ref[0, 1, i].astype(f32) * high_t[:, i:i + 1]
        turned_ref[:, i, :] = jnp.where(lane < bins, low, high)
    n_cols_piece = n_cols // n_parts
    for turn in range(len(outs) // n_parts):
        @pl.when(pl.program_id(0) == turn)
        def _(turn=turn):
            for part in range(n_parts):
                start = (part + idx_ref[0]) % n_parts * n_cols_piece
                outs[turn * n_parts + part][...] = turned_ref[pl.ds(start, n_cols_piece)].astype(bf16)


def gates(both):
    hidden = both.shape[1] // 2
    up_pre, gate_pre = both[:, :hidden], both[:, hidden:]
    sigma = jnp.tanh(gate_pre * 0.5) * 0.5 + 0.5
    silu = gate_pre * sigma
    return up_pre, sigma, silu, silu * up_pre


def forward_kernel(
    span, n_given, pair_ref, row_ref, col_ref, rpos_ref, cpos_ref, table_ref, up_gate_ref, down_ref, *refs
):
    both_ref, norm_ref, norm_t_ref, inv_ref, out_t_ref = refs[n_given:]
    n_cols, width = pair_ref.shape[1:]
    n_rows = min(pair_ref.shape[0], 1024 // n_cols)
    count = n_rows * n_cols
    for sub in range(pair_ref.shape[0] // n_rows):
        rows = slice(sub * n_rows, (sub + 1) * n_rows)
        flat = slice(sub * count, (sub + 1) * count)
        offset = jnp.clip(rpos_ref[rows][:, None, :] - cpos_ref[...][None, :, :], -span, span) + span
        lane = lax.broadcasted_iota(jnp.int32, offset.shape, 2)
        hot = jnp.where(offset == lane, 1.0, 0.0).astype(bf16).reshape(count, lanes)
        pair_in = pair_ref[rows].astype(f32) + row_ref[rows][:, None, :] + col_ref[...][None, :, :]
        pair_in = pair_in.reshape(count, width) + product(hot, table_ref[...])
        centred = pair_in - jnp.mean(pair_in, axis=-1, keepdims=True)
        inv_std = lax.rsqrt(jnp.mean(centred * centred, axis=-1, keepdims=True) + norm_eps)
        normed_bf = (centred * inv_std).astype(bf16)
        norm_ref[flat] = normed_bf
        norm_t_ref[0, :, flat] = normed_bf.T
        inv_ref[flat] = jnp.broadcast_to(inv_std, (count, width)).astype(bf16)
        both = product(normed_bf, up_gate_ref[...]).astype(bf16)
        both_ref[flat] = both
        hid = gates(both)[3]
        pair_out = (pair_in + product(hid, down_ref[...])).astype(bf16)
        out_t_ref[0, :, flat] = pair_out.T


def backward_kernel(n_pieces, n_given, n_chained, idx_ref, cot_ref, mask_ref, *refs):
    mirror_refs = refs[:n_pieces]
    (both_ref, norm_ref, norm_t_ref, inv_ref, out_t_ref, bucket_ref,
     head_t_ref, down_t_ref, up_t_ref, gate_t_ref) = refs[n_pieces:n_pieces + 10]
    before = refs[n_pieces + 10 + n_given:n_pieces + 10 + n_given + n_chained]
    refs = refs[n_pieces + 10 + n_given + n_chained:]
    grad_ref, rows_ref, cols_ref, sums_ref, mir_ref, ug_acc, down_acc, head_acc, rel_acc, cols_acc = refs
    piece = pl.program_id(0)
    step = pl.program_id(1)
    first = (piece == 0) & (step == 0)
    last = (piece == pl.num_programs(0) - 1) & (step == pl.num_programs(1) - 1)
    n_cols, width = cot_ref.shape[1:]
    n_rows = min(cot_ref.shape[0], 1024 // n_cols)
    count = n_rows * n_cols
    half = n_cols // 2
    hidden = down_t_ref.shape[1]
    bins = width // 2

    n_slabs = hidden // lanes

    @pl.when(first)
    def _():
        if before:
            cols_acc[...] = before[0][...]
            for q in range(2 * n_slabs):
                ug_acc[:, q * lanes:(q + 1) * lanes] = before[1][q]
            for q in range(n_slabs):
                down_acc[:, q * lanes:(q + 1) * lanes] = before[1][2 * n_slabs + q].T
            head_acc[...] = before[1][3 * n_slabs]
            rel_acc[...] = before[1][3 * n_slabs + 1]
        else:
            for acc in (cols_acc, ug_acc, down_acc, head_acc, rel_acc):
                acc[...] = jnp.zeros_like(acc)

    for t in range(n_pieces):
        @pl.when(piece == t)
        def _(t=t):
            mir_ref[...] = mirror_refs[t][...]

    for sub in range(cot_ref.shape[0] // n_rows):
        rows = slice(sub * n_rows, (sub + 1) * n_rows)
        flat = slice(sub * count, (sub + 1) * count)
        packed = mir_ref[rows].astype(f32).reshape(n_rows * half, width)
        turned = pltpu.roll(packed, bins, 1).reshape(n_rows, half, width)
        mirrored = jnp.concatenate([turned, packed.reshape(n_rows, half, width)], axis=1)
        lane = lax.broadcasted_iota(jnp.int32, mirrored.shape, 2)
        mask_t = mask_ref[rows].astype(f32).T
        own = jnp.stack([cot_ref[sub * n_rows + i].astype(f32) * mask_t[:, i:i + 1] for i in range(n_rows)], axis=0)
        head_cot = (own + jnp.where(lane >= bins, mirrored, 0.0)).astype(bf16).reshape(count, width)
        grad_out = product(head_cot, head_t_ref[...])
        grad_out_bf = grad_out.astype(bf16)
        grad_hid = product(grad_out_bf, down_t_ref[...]).astype(bf16)
        up_pre, sigma, silu, hid = gates(both_ref[flat])
        grad_up = grad_hid * silu
        grad_gate = grad_hid * (up_pre * (sigma + silu * (1.0 - sigma)))
        grad_normed = product(grad_up, up_t_ref[...]) + product(grad_gate, gate_t_ref[...])
        normed = norm_ref[flat].astype(f32)
        grad_in = grad_out + inv_ref[flat].astype(f32) * (
            grad_normed
            - jnp.mean(grad_normed, axis=-1, keepdims=True)
            - normed * jnp.mean(grad_normed * normed, axis=-1, keepdims=True)
        )
        grad_tile = grad_in.reshape(n_rows, n_cols, width)
        grad_bf = grad_in.astype(bf16)
        grad_ref[rows] = grad_bf.reshape(n_rows, n_cols, width)
        rows_ref[rows] = jnp.sum(grad_tile, axis=1).astype(rows_ref.dtype)
        cols_acc[...] += jnp.sum(grad_tile, axis=0)
        norm_t = norm_t_ref[0, :, flat]
        ug_acc[:, :hidden] += product(norm_t, grad_up)
        ug_acc[:, hidden:] += product(norm_t, grad_gate)
        down_acc[...] += product(grad_out_bf.T, hid)
        head_acc[...] += product(out_t_ref[0, :, flat], head_cot)
        level = lax.broadcasted_iota(jnp.int32, (lanes, count), 0)
        bucket = jnp.broadcast_to(bucket_ref[0, :, flat], (lanes, count))
        rel_acc[...] += product(jnp.where(bucket == level, 1.0, 0.0).astype(bf16), grad_bf)

    @pl.when(last)
    def _():
        cols_ref[...] = cols_acc[...].astype(cols_ref.dtype)
        slabs = [ug_acc[:, q * lanes:(q + 1) * lanes] for q in range(2 * n_slabs)]
        slabs += [down_acc[:, q * lanes:(q + 1) * lanes].T for q in range(n_slabs)]
        for q, slab in enumerate(slabs + [head_acc[...], rel_acc[...]]):
            sums_ref[q] = slab.astype(sums_ref.dtype)


def unpack_kernel(slabs_ref, up_ref, gate_ref, down_ref, head_ref, rel_ref):
    n_slabs = up_ref.shape[1] // lanes
    for q in range(n_slabs):
        at = slice(q * lanes, (q + 1) * lanes)
        up_ref[:, at] = slabs_ref[q].astype(f32)
        gate_ref[:, at] = slabs_ref[n_slabs + q].astype(f32)
        down_ref[at] = slabs_ref[2 * n_slabs + q].astype(f32)
    head_ref[...] = slabs_ref[3 * n_slabs].astype(f32)
    rel_ref[...] = slabs_ref[3 * n_slabs + 1, :rel_ref.shape[0]].astype(f32)


def transition(tokens_in, single_gate, single_up, single_down):
    src = tokens_in.astype(f32)
    inv_rms = lax.rsqrt(jnp.mean(src * src, axis=-1, keepdims=True) + norm_eps)
    normed_bf = (src * inv_rms).astype(bf16)
    silu, _ = gated_parts(product(normed_bf, single_gate))
    hid = (silu * product(normed_bf, single_up)).astype(bf16)
    updated = (src + product(hid, single_down)).astype(bf16)
    return normed_bf, hid, updated


def gather_all(piece, n_dev):
    copies = jnp.broadcast_to(piece[None], (n_dev,) + piece.shape)
    return lax.all_to_all(copies, axes, split_axis=0, concat_axis=0, tiled=True)


def local(
    pair_repr, logit_cotangent, pair_mask, single_repr, token_index, pair_up, pair_gate, pair_down, head_weight,
    rel_table, proj_row, proj_col, single_gate, single_up, single_down,
):
    n_row = lax.axis_size("row")
    n_col = lax.axis_size("col")
    n_dev = n_row * n_col
    fold = n_col // n_row
    row_index = lax.axis_index("row")
    col_index = lax.axis_index("col")
    joint_index = row_index * n_col + col_index
    core = col_index % fold
    tile_rows, tile_cols, width = pair_repr.shape
    half = tile_cols // 2
    strip = single_repr.shape[0]
    tokens = strip * n_dev
    hidden = pair_up.shape[1]
    s_hidden = single_gate.shape[1]
    share = s_hidden // n_dev
    n_rel = rel_table.shape[0]
    span = (n_rel - 1) // 2
    n_groups = 2 if n_row % 2 == 0 else 1
    per_turn = n_row // fold
    piece_rows = tile_cols // per_turn
    block_rows = min(2048 // tile_cols, piece_rows)
    count = block_rows * tile_cols
    n_blocks = tile_rows // block_rows
    n_slabs = hidden // lanes
    n_sums = 3 * n_slabs + 2

    core_arr = core.astype(jnp.int32).reshape(1)
    n_parts = per_turn
    group = 16
    blocks = half // group

    def part_map(s, i, idx):
        return ((idx[0] + s) % fold, 0, i, 0, 0)

    def sent_map(s, i, idx, own=0):
        return (0, jnp.where(s == own, i, jnp.where(s < own, 0, blocks - 1)), 0)

    parted = (fold, 2, half, tile_cols)
    prepared = pl.pallas_call(
        functools.partial(prepare_kernel, n_parts),
        grid_spec=pltpu.PrefetchScalarGridSpec(
            num_scalar_prefetch=1,
            grid=(fold, blocks),
            in_specs=[
                pl.BlockSpec((1, 2, group, tile_cols, width), part_map),
                pl.BlockSpec((1, 2, group, tile_cols), lambda s, i, idx: part_map(s, i, idx)[:4]),
            ],
            out_specs=[
                pl.BlockSpec((piece_rows, group, width), functools.partial(sent_map, own=t // n_parts))
                for t in range(fold * n_parts)
            ],
            scratch_shapes=[pltpu.VMEM((tile_cols, group, width), f32)],
        ),
        out_shape=[jax.ShapeDtypeStruct((piece_rows, half, width), bf16)] * (fold * n_parts),
        cost_estimate=pl.CostEstimate(
            flops=tile_rows * tile_cols * width * 4, bytes_accessed=tile_rows * tile_cols * width * 3, transcendentals=0
        ),
        name="mask_and_turn",
    )(core_arr, logit_cotangent.reshape(parted + (width,)), pair_mask.reshape(parted))
    sent = prepared

    def place(r, k, b):
        return r * n_col + k * fold + b

    every = [(r, k, b) for r in range(n_row) for k in range(n_row) for b in range(fold)]

    def by_way(u, r, k, b):
        return (r + k + u // per_turn * per_turn + (u % per_turn + b) % per_turn) % n_row

    def onward(u):
        s = u // per_turn
        return [(place(by_way(u, r, k, b), k, b), place(k, r, (b + s) % fold)) for r, k, b in every]

    order = [t for group_no in range(n_groups) for t in range(group_no, n_row, n_groups)]
    pieces = {}
    for t in order:
        spread = [(place(r, k, b), place(by_way(t, r, k, b), k, b)) for r, k, b in every]
        pieces[t] = lax.ppermute(sent[t], axes, spread)
    singles = gather_all(single_repr, n_dev).reshape(tokens, -1)

    row_pos = lax.dynamic_slice_in_dim(token_index, row_index * tile_rows, tile_rows, 0)
    col_pos = lax.dynamic_slice_in_dim(token_index, col_index * tile_cols, tile_cols, 0)
    rpos = jnp.broadcast_to(row_pos[:, None], (tile_rows, lanes))
    cpos = jnp.broadcast_to(col_pos[:, None], (tile_cols, lanes))
    bucket = (jnp.clip(row_pos[:, None] - col_pos[None, :], -span, span) + span).reshape(n_blocks, 1, count)
    table = jnp.pad(rel_table, ((0, lanes - n_rel), (0, 0)))
    up_gate = jnp.concatenate([pair_up, pair_gate], axis=1)

    singles, rpos, cpos, bucket, table, up_gate = lax.optimization_barrier(
        (singles, rpos, cpos, bucket, table, up_gate)
    )
    near = jnp.concatenate(
        [
            lax.dynamic_slice_in_dim(singles, row_index * tile_rows, tile_rows, 0),
            lax.dynamic_slice_in_dim(singles, col_index * tile_cols, tile_cols, 0),
        ],
        axis=0,
    )
    near_updated = transition(near, single_gate, single_up, single_down)[2]
    row_proj = product(near_updated[:tile_rows], proj_row).astype(bf16).astype(f32)
    col_proj = product(near_updated[tile_rows:], proj_col).astype(bf16).astype(f32)

    n_pairs = tile_rows * tile_cols
    whole = lambda shape: pl.BlockSpec(shape, lambda *_: (0,) * len(shape))
    flat = lambda cols_, where: pl.BlockSpec((count, cols_), lambda *at: (where(*at), 0))
    lead = lambda shape, where: pl.BlockSpec((1,) + shape, lambda *at: (where(*at), 0, 0))
    tile = lambda where: pl.BlockSpec((block_rows, tile_cols, width), lambda *at: (where(*at), 0, 0))
    some = lambda cols_, where: pl.BlockSpec((block_rows, cols_), lambda *at: (where(*at), 0))
    saved = ()
    held = pieces
    pieces = {}
    cuts = (0, n_blocks * 3 // 8, n_blocks * 13 // 16, n_blocks)
    for low, high in zip(cuts[:-1], cuts[1:]):
        part = lambda i, low=low: i + low
        operands = [pair_repr, row_proj, col_proj, rpos, cpos, table, up_gate, pair_down]
        saved = pl.pallas_call(
            functools.partial(forward_kernel, span, len(saved)),
            grid=(high - low,),
            in_specs=[
                tile(part), some(width, part), whole((tile_cols, width)), some(lanes, part), whole((tile_cols, lanes)),
                whole(table.shape), whole(up_gate.shape), whole(pair_down.shape),
            ]
            + [pl.BlockSpec(memory_space=pl.ANY)] * len(saved),
            out_specs=[
                flat(2 * hidden, part), flat(width, part), lead((width, count), part), flat(width, part),
                lead((width, count), part),
            ],
            out_shape=[
                jax.ShapeDtypeStruct((n_pairs, 2 * hidden), bf16),
                jax.ShapeDtypeStruct((n_pairs, width), bf16),
                jax.ShapeDtypeStruct((n_blocks, width, count), bf16),
                jax.ShapeDtypeStruct((n_pairs, width), bf16),
                jax.ShapeDtypeStruct((n_blocks, width, count), bf16),
            ],
            input_output_aliases={len(operands) + i: i for i in range(len(saved))},
            cost_estimate=pl.CostEstimate(
                flops=2 * n_pairs * width * (3 * hidden + lanes) * (high - low) // n_blocks,
                bytes_accessed=n_pairs * (4 * hidden + 10 * width) * (high - low) // n_blocks,
                transcendentals=n_pairs * hidden * (high - low) // n_blocks,
            ),
            name="pair_forward",
        )(*operands, *saved)
        number = cuts.index(low)
        if number < 2:
            held, inv_held = lax.optimization_barrier((held, saved[3]))
            saved = list(saved[:3]) + [inv_held] + list(saved[4:])
            for t in range(number, n_row, 2):
                pieces[t] = lax.ppermute(held[t], axes, onward(t))

    head_t = head_weight.T
    down_t = pair_down.T
    up_t = pair_up.T
    gate_t = pair_gate.T
    steps = piece_rows // block_rows
    n_pieces = n_row // n_groups
    given, chained = (), ()
    for group_no in range(n_groups):
        def block_of(p, j, idx, group_no=group_no):
            t = p * n_groups + group_no
            strip_no = (idx[0] + fold - t // per_turn) % fold
            return strip_no * (tile_cols // block_rows) + (t % per_turn + strip_no) % per_turn * steps + j

        def mirror_map(p, j, idx, own=0):
            return (jnp.where(p == own, j, jnp.where(p < own, 0, steps - 1)), 0, 0)

        in_specs = (
            [tile(block_of), some(tile_cols, block_of)]
            + [
                pl.BlockSpec((block_rows, half, width), functools.partial(mirror_map, own=p))
                for p in range(n_pieces)
            ]
            + [flat(2 * hidden, block_of), flat(width, block_of), lead((width, count), block_of),
               flat(width, block_of), lead((width, count), block_of), lead((1, count), block_of),
               whole(head_t.shape), whole(down_t.shape), whole(up_t.shape), whole(gate_t.shape)]
            + [pl.BlockSpec(memory_space=pl.ANY)] * len(given)
            + [whole(x.shape) for x in chained]
        )
        operands = [logit_cotangent, pair_mask] + [pieces[p * n_groups + group_no] for p in range(n_pieces)] + list(saved) + [
            bucket, head_t, down_t, up_t, gate_t] + list(given) + list(chained)
        first_given = 1 + len(operands) - len(given) - len(chained)
        kept = bf16 if group_no == n_groups - 1 else f32
        pair_grad, row_part, cols, sums = pl.pallas_call(
            functools.partial(backward_kernel, n_pieces, len(given), len(chained)),
            grid_spec=pltpu.PrefetchScalarGridSpec(
                num_scalar_prefetch=1,
                grid=(n_pieces, steps),
                in_specs=in_specs,
                out_specs=[
                    tile(block_of), some(width, block_of), whole((tile_cols, width)), whole((n_sums, lanes, lanes)),
                ],
                scratch_shapes=[
                    pltpu.VMEM((block_rows, half, width), bf16),
                    pltpu.VMEM((width, 2 * hidden), f32),
                    pltpu.VMEM((width, hidden), f32),
                    pltpu.VMEM((width, lanes), f32),
                    pltpu.VMEM((lanes, width), f32),
                    pltpu.VMEM((tile_cols, width), f32),
                ],
            ),
            out_shape=[
                jax.ShapeDtypeStruct(pair_repr.shape, bf16),
                jax.ShapeDtypeStruct((tile_rows, width), bf16),
                jax.ShapeDtypeStruct((tile_cols, width), kept),
                jax.ShapeDtypeStruct((n_sums, lanes, lanes), kept),
            ],
            input_output_aliases={first_given + i: i for i in range(len(given))},
            cost_estimate=pl.CostEstimate(
                flops=2 * n_pairs * width * (6 * hidden + 3 * lanes) // n_groups,
                bytes_accessed=n_pairs * (4 * hidden + 13 * width) // n_groups,
                transcendentals=n_pairs * hidden // n_groups,
            ),
            name="pair_backward",
        )(core_arr, *operands)
        given, chained = (pair_grad, row_part), (cols, sums)

    sum_rows = n_sums * lanes // n_dev

    def spread_out(part):
        size = part.size // n_dev
        narrow = min(size, lanes)
        return jnp.pad(part.reshape(n_dev, size // narrow, narrow), ((0, 0), (0, 0), (0, lanes - narrow)))

    row_sent, col_sent = spread_out(row_part), spread_out(cols)
    row_len, col_len = row_sent.shape[1], col_sent.shape[1]
    outgoing = jnp.concatenate([sums.reshape(n_dev, sum_rows, lanes), row_sent, col_sent], axis=1)
    outgoing, singles = lax.optimization_barrier((outgoing, singles))
    s_normed_bf, _, updated = transition(singles, single_gate, single_up, single_down)
    arrived = lax.all_to_all(outgoing, axes, split_axis=0, concat_axis=0, tiled=True).astype(f32)
    row_own = jnp.sum(arrived[:, sum_rows:sum_rows + row_len].reshape(n_row, n_col, row_len, lanes), axis=1)
    col_own = jnp.sum(arrived[:, sum_rows + row_len:].reshape(n_row, n_col, col_len, lanes), axis=0)
    totals = jnp.concatenate(
        [row_own.reshape(n_row * row_len, lanes), col_own.reshape(n_col * col_len, lanes)], axis=0
    ).astype(bf16)
    grad_scale = 1.0 / tokens
    own_sums = (jnp.sum(arrived[:, :sum_rows], axis=0) * grad_scale).astype(bf16)
    totals_all = gather_all(totals, n_dev)
    own_sums, totals_all = lax.optimization_barrier((own_sums, totals_all))
    shared = gather_all(own_sums, n_dev)
    slabs = shared.reshape(n_sums, lanes, lanes)

    def tokens_of(held, n_strips, length):
        used = tokens * width // (n_strips * n_dev * length)
        return held.reshape(n_dev, n_strips, length, lanes)[..., :used].transpose(1, 0, 2, 3).reshape(tokens, width)

    row_bf = tokens_of(totals_all[:, :n_row * row_len], n_row, row_len)
    col_bf = tokens_of(totals_all[:, n_row * row_len:], n_col, col_len)

    single_cot = product_right(row_bf, proj_row) + product_right(col_bf, proj_col)
    cot_bf = single_cot.astype(bf16)
    prow_sum = product_left(updated, row_bf)
    pcol_sum = product_left(updated, col_bf)
    gate_cols = lax.dynamic_slice_in_dim(single_gate, joint_index * share, share, 1)
    up_cols = lax.dynamic_slice_in_dim(single_up, joint_index * share, share, 1)
    down_rows = lax.dynamic_slice_in_dim(single_down, joint_index * share, share, 0)
    own_up = product(s_normed_bf, up_cols)
    own_silu, own_slope = gated_parts(product(s_normed_bf, gate_cols))
    own_hid = (own_silu * own_up).astype(bf16)
    own_grad_hid = product_right(cot_bf, down_rows)
    own_grad_up = (own_grad_hid * own_silu).astype(bf16)
    own_grad_gate = (own_grad_hid * own_up * own_slope).astype(bf16)
    gate_sum = product_left(s_normed_bf, own_grad_gate)
    up_sum = product_left(s_normed_bf, own_grad_up)
    down_sum = product_left(own_hid, cot_bf)

    mine = lambda whole_: lax.dynamic_slice_in_dim(whole_, joint_index * strip, strip, 0)
    my_src = single_repr.astype(f32)
    my_inv = lax.rsqrt(jnp.mean(my_src * my_src, axis=-1, keepdims=True) + norm_eps)
    my_normed = my_src * my_inv
    my_normed_bf = my_normed.astype(bf16)
    my_up = product(my_normed_bf, single_up)
    my_silu, my_slope = gated_parts(product(my_normed_bf, single_gate))
    my_cot = mine(single_cot)
    my_grad_hid = product_right(my_cot.astype(bf16), single_down)
    my_grad_up = (my_grad_hid * my_silu).astype(bf16)
    my_grad_gate = (my_grad_hid * my_up * my_slope).astype(bf16)
    my_grad_normed = product_right(my_grad_gate, single_gate) + product_right(my_grad_up, single_up)
    single_grad = my_cot + my_inv * (
        my_grad_normed - my_normed * jnp.mean(my_grad_normed * my_normed, axis=-1, keepdims=True)
    )

    pair_sums = pl.pallas_call(
        unpack_kernel,
        out_shape=[
            jax.ShapeDtypeStruct(pair_up.shape, f32),
            jax.ShapeDtypeStruct(pair_gate.shape, f32),
            jax.ShapeDtypeStruct(pair_down.shape, f32),
            jax.ShapeDtypeStruct(head_weight.shape, f32),
            jax.ShapeDtypeStruct(rel_table.shape, f32),
        ],
        name="unpack_sums",
    )(slabs)
    return (
        pair_grad,
        single_grad.astype(bf16),
        *pair_sums,
        prow_sum * grad_scale,
        pcol_sum * grad_scale,
        gate_sum * grad_scale,
        up_sum * grad_scale,
        down_sum * grad_scale,
    )


def solution(mesh):
    placed = (
        P("row", "col", None),
        P("row", "col", None),
        P("row", "col"),
        P(("row", "col"), None),
    ) + (P(),) * 11
    return jax.shard_map(
        local,
        mesh=mesh,
        in_specs=placed,
        out_specs=(P("row", "col", None), P(("row", "col"), None))
        + (P(),) * 7
        + (P(None, ("row", "col")), P(None, ("row", "col")), P(("row", "col"), None)),
        check_vma=False,
    )
```
